32 devices in a mesh: groups: 2 (over y), level: 4 (over z), src: 2 (over x), phase: 2 (over core).
Axes of the slice: x: 2, y: 2, z: 4, core: 2. Of those that a mesh axis runs over, the one named last changes fastest.
Arguments:
- state_values: float32 [24, 8, 32, 16, 128], P(('groups', 'level'), 'src', 'phase'), parts along dimension 0, may hold values from -6 to 6
- phase_rates: float32 [64, 32], P('groups'), parts along dimension 0, may hold values from 0.05 to 2
- batch_rates: float32 [32, 32, 32], P('groups'), parts along dimension 0, may hold values from 0.02 to 1
- service_rates: float32 [4], P('groups'), parts along dimension 0, may hold values from 20 to 60
- source_rates: float32 [6, 3], P('groups'), parts along dimension 0, may hold values from 2 to 30
- tile_levels: int32 [16, 2], P('groups'), parts along dimension 0, may hold values from 0 to 3, as said below
- routes: int32 [16, 5], P('groups'), parts along dimension 0, may hold values from -1 to 7, as said below
- tile_owner: int32 [16], P('groups'), parts along dimension 0, may hold values from 0 to 11, as said below
Outputs:
- stepped_values: float32 [24, 8, 32, 16, 128], P(('groups', 'level'), 'src', 'phase'), parts along dimension 0
The draws below stay inside these ranges and needn't reach their ends.
There are 2 independent parts, one for each index of `groups`. The reference program is written for one: setup_inputs(seed, part) draws one part's arguments, and reference() takes and returns one part's arrays. A program takes and returns all parts, laid end to end along the dimension named above; each array names one. Nothing has to cross between parts.
Inputs may be any that keep to these rules, and one draw needn't show every extreme that they name: `tile_levels`: row t is the tile (a, c) covering buffer-one levels a * 128 to a * 128 + 127 and buffer-two levels c * 16 to c * 16 + 15; tiles are numbered column by column (c rising, then a rising), every c from 0 to 3 has tiles a = 0, 1, ... up to its own height, and the tallest column has 3 tiles. routes[t] lists the tiles (a - 1, c), (a + 1, c), (a, c - 1), (a, c + 1) and (a + 1, c - 1) of tile t = (a, c), or -1 where no such tile exists. `tile_owner`: each tile has its own slot; slots d * 3 to d * 3 + 2 belong to index d of level. Every index holds 1 to 3 tiles, the busiest exactly 3, with consecutive tile numbers in its first slots in order. Slots that hold no tile are ignored.
All inputs are finite; a program needn't handle non-finite values.
Results may differ from the reference program's by a relative error of at most 0.0001.
Values sent between devices are 32-bit elements; how exact they have to be, the bound alone decides.
No kernel may reach another device: no remote copies, remote signals or barrier semaphores. Data moves between devices by JAX's collectives and lax.ppermute only.
A program may use at most 128 MiB of HBM per device.

```python
import math
import jax
import jax.numpy as jnp
from jax import lax

P_SIZE = 32
BATCH = 16
SOURCES = 3
STATES = 8
TB1 = 128
TB2 = 16
MEAN_TILES = 2
CAP = 3
TILES = 8
COLS = 4
SLOTS = 12
N_LEVEL = 4


def pair_counts(key, groups, mean_size):
    perm_key, spread_key = jax.random.split(key)
    shuffled = jax.random.permutation(perm_key, groups)
    spread = jax.random.randint(spread_key, (groups // 2,), 0, mean_size)
    spread = spread.at[0].set(mean_size - 1)
    values = jnp.concatenate([mean_size + spread, mean_size - spread]).astype(jnp.int32)
    return jnp.zeros((groups,), jnp.int32).at[shuffled].set(values)


def tile_layout(key):
    base_key = jax.random.fold_in(key, 5)
    cols_key, devs_key, shuffle_key = jax.random.split(base_key, 3)
    heights = pair_counts(cols_key, COLS, MEAN_TILES)
    counts = pair_counts(devs_key, N_LEVEL, MEAN_TILES)
    device_order = jax.random.permutation(shuffle_key, N_LEVEL).astype(jnp.int32)
    busiest = jnp.argmax(counts).astype(jnp.int32)
    last_at = jnp.argmax(device_order == N_LEVEL - 1).astype(jnp.int32)
    moved_device = device_order[busiest]
    device_order = device_order.at[last_at].set(moved_device).at[busiest].set(N_LEVEL - 1).astype(jnp.int32)
    tile_ids = jnp.arange(TILES, dtype=jnp.int32)
    column_end = jnp.cumsum(heights).astype(jnp.int32)
    column_start = column_end - heights
    column = jnp.sum((column_end[None, :] <= tile_ids[:, None]).astype(jnp.int32), axis=1).astype(jnp.int32)
    tier_pos = tile_ids - column_start[column]
    height_here = heights[column]
    left_col = jnp.maximum(column - 1, 0)
    right_col = jnp.minimum(column + 1, COLS - 1)
    from_below = jnp.where(tier_pos > 0, tile_ids - 1, -1)
    from_above = jnp.where(tier_pos + 1 < height_here, tile_ids + 1, -1)
    from_left = jnp.where((column > 0) & (tier_pos < heights[left_col]), column_start[left_col] + tier_pos, -1)
    from_right = jnp.where((column + 1 < COLS) & (tier_pos < heights[right_col]), column_start[right_col] + tier_pos, -1)
    corner = jnp.where((column > 0) & (tier_pos + 1 < heights[left_col]), column_start[left_col] + tier_pos + 1, -1)
    routes = jnp.stack([from_below, from_above, from_left, from_right, corner], axis=1).astype(jnp.int32)
    range_end = jnp.cumsum(counts).astype(jnp.int32)
    range_start = range_end - counts
    holder = jnp.sum((range_end[None, :] <= tile_ids[:, None]).astype(jnp.int32), axis=1).astype(jnp.int32)
    owner = (device_order[holder] * CAP + tile_ids - range_start[holder]).astype(jnp.int32)
    levels = jnp.stack([tier_pos, column], axis=1).astype(jnp.int32)
    return (levels, routes, owner)


def draw_tile_levels(key, part):
    return tile_layout(key)[0]


def draw_routes(key, part):
    return tile_layout(key)[1]


def draw_tile_owner(key, part):
    return tile_layout(key)[2]


def level_of(key, extent, shards, least, top_value):
    def one(position, shards_of):
        steps = jax.random.uniform(jax.random.fold_in(jax.random.fold_in(key, 6), position), (shards_of,), jnp.float32, least / len(shards), top_value / len(shards))
        return jnp.repeat(jnp.exp(steps), extent[position] // shards_of).reshape((-1,) + (1,) * (len(extent) - position - 1))

    level = one(*shards[0])
    for cut in shards[1:]:
        level = level * one(*cut)
    return level


def normal_values(rng, extent, scale, limit, pieces=(), held_as=jnp.bfloat16):
    values = scale * jax.random.normal(rng, extent, jnp.float32)
    if pieces:
        values = values * level_of(rng, extent, pieces, -0.22, 0.18)
    return jnp.clip(values, -limit, limit).astype(held_as)


def setup_inputs(seed: int = 0, part: int = 0) -> dict:
    seeds = jax.random.split(jax.random.key(seed), 9)
    own_keys = jax.random.split(jax.random.fold_in(seeds[8], part), 9)
    return {
        "state_values": normal_values(own_keys[0], (SLOTS, STATES, P_SIZE, TB2, TB1), 1.0, 6.0, ((0, 4), (1, 2), (2, 2)), jnp.float32),
        "phase_rates": jnp.clip(jnp.exp(jax.random.uniform(own_keys[1], (P_SIZE, P_SIZE), jnp.float32, math.log(0.05), math.log(2.0))), 0.05, 2.0),
        "batch_rates": jnp.clip(jnp.exp(jax.random.uniform(own_keys[2], (BATCH, P_SIZE, P_SIZE), jnp.float32, math.log(0.02), math.log(1.0))), 0.02, 1.0),
        "service_rates": jnp.clip(jnp.exp(jax.random.uniform(own_keys[3], (2,), jnp.float32, math.log(20.0), math.log(60.0))), 20.0, 60.0),
        "source_rates": jnp.clip(jnp.exp(jax.random.uniform(own_keys[4], (SOURCES, 3), jnp.float32, math.log(2.0), math.log(30.0))), 2.0, 30.0),
        "tile_levels": draw_tile_levels(jax.random.fold_in(jax.random.fold_in(seeds[8], part), 71), part),
        "routes": draw_routes(jax.random.fold_in(jax.random.fold_in(seeds[8], part), 71), part),
        "tile_owner": draw_tile_owner(jax.random.fold_in(jax.random.fold_in(seeds[8], part), 71), part),
    }


PRECISE = lax.Precision.HIGHEST


def phase_tables(phase_rates, batch_rates):
    phases = phase_rates.shape[0]
    unit_matrix = jnp.eye(phases, dtype=phase_rates.dtype)
    moving = phase_rates * (1.0 - unit_matrix)
    leaving = jnp.sum(moving, axis=1) + jnp.sum(batch_rates, axis=(0, 2))
    stacked = jnp.concatenate([(moving - unit_matrix * leaving[:, None])[None], batch_rates], axis=0)
    return stacked, jnp.max(leaving)


def uniform_rate(top_leaving, service_rates, source_rates):
    sources_top = jnp.sum(jnp.maximum(source_rates[:, 2] + source_rates[:, 1], source_rates[:, 0]))
    return top_leaving + service_rates[0] + service_rates[1] + sources_top


def source_terms(states, source_rates):
    powers = jnp.cumprod(jnp.full((SOURCES,), 2, jnp.int32)) // 2
    on_bits = ((states[:, None] // powers[None, :]) % 2).astype(source_rates.dtype)
    turn_on = source_rates[:, 0][None, :]
    turn_off = source_rates[:, 1][None, :]
    arrive = source_rates[:, 2][None, :]
    feeding = jnp.sum(on_bits * arrive, axis=1)
    incoming = on_bits * turn_on + (1.0 - on_bits) * turn_off
    outgoing = jnp.sum(on_bits * turn_off + (1.0 - on_bits) * turn_on, axis=1)
    return feeding, incoming, outgoing


def product(tile_data, tile_levels, routes, tables, uniform, service_rates, feeding, incoming, outgoing):
    target = jnp.maximum(routes, 0)
    present = routes >= 0
    top_rim = jnp.where(present[:, 0][:, None, None, None, None], tile_data[target[:, 0], :, :, :, TB1 - BATCH:], 0.0)
    above_bottom = jnp.where(present[:, 1][:, None, None, None], tile_data[target[:, 1], :, :, :, 0], 0.0)
    left_last = jnp.where(present[:, 2][:, None, None, None], tile_data[target[:, 2], :, :, TB2 - 1, :], 0.0)
    right_first = jnp.where(present[:, 3][:, None, None, None], tile_data[target[:, 3], :, :, 0, :], 0.0)
    corner_cell = jnp.where(present[:, 4][:, None, None], tile_data[target[:, 4], :, :, TB2 - 1, 0], 0.0)
    extended = jnp.concatenate([top_rim, tile_data], axis=-1)
    change = jnp.zeros_like(tile_data)
    for offset in range(BATCH + 1):
        window = extended[..., BATCH - offset:BATCH - offset + TB1]
        change = change + jnp.einsum("rspuv,pq->rsquv", window, tables[offset], precision=PRECISE)
    row_ext = jnp.concatenate([tile_data, above_bottom[..., None]], axis=-1)
    side_ext = jnp.concatenate([left_last, corner_cell[..., None]], axis=-1)
    joined = jnp.concatenate([side_ext[..., None, :], row_ext], axis=-2)
    service_one = joined[..., :TB2, 1:]
    service_two = jnp.concatenate([tile_data, right_first[..., None, :]], axis=-2)[..., 1:, :]
    feed_two = jnp.concatenate([left_last[..., None, :], tile_data], axis=-2)[..., :TB2, :]
    for source_bit in range(SOURCES):
        stride = 2 ** source_bit
        shaped = tile_data.reshape((tile_data.shape[0], STATES // (2 * stride), 2, stride) + tile_data.shape[2:])
        partner = jnp.flip(shaped, axis=2).reshape(tile_data.shape)
        change = change + incoming[:, source_bit][None, :, None, None, None] * partner
    first_pos = (tile_levels[:, 0][:, None] * TB1 + jnp.arange(TB1, dtype=jnp.int32)[None, :]) > 0
    second_pos = (tile_levels[:, 1][:, None] * TB2 + jnp.arange(TB2, dtype=jnp.int32)[None, :]) > 0
    leaving_rate = (service_rates[0] * first_pos[:, None, None, None, :]
                    + service_rates[1] * second_pos[:, None, None, :, None]
                    + (feeding + outgoing)[None, :, None, None, None])
    change = (change + service_rates[0] * service_one + service_rates[1] * service_two
              + feeding[None, :, None, None, None] * feed_two - leaving_rate * tile_data)
    return tile_data + change / uniform


def reference(state_values, phase_rates, batch_rates, service_rates, source_rates, tile_levels, routes, tile_owner):
    tables, top_leaving = phase_tables(phase_rates, batch_rates)
    uniform = uniform_rate(top_leaving, service_rates, source_rates)
    states = jnp.arange(STATES, dtype=jnp.int32)
    feeding, incoming, outgoing = source_terms(states, source_rates)
    tile_data = state_values[tile_owner]
    for repeat in range(2):
        tile_data = product(tile_data, tile_levels, routes, tables, uniform, service_rates, feeding, incoming, outgoing)
    return jnp.zeros_like(state_values).at[tile_owner].set(tile_data)
```

```python
import functools

import jax
import jax.numpy as jnp
from jax import lax
from jax.experimental import pallas as pl
from jax.experimental.pallas import tpu as pltpu
from jax.sharding import PartitionSpec as P

BATCH = 16
SOURCES = 3
LANES = 128
F32 = jnp.float32
BF16 = jnp.bfloat16
VM = pltpu.VMEM
SM = pltpu.SMEM


def shift_from(x, axis, step):
    n = lax.axis_size(axis)
    return lax.ppermute(x, axis, [((i + step) % n, i) for i in range(n)])


def from_partner(x, axis, bit):
    return lax.ppermute(x, axis, [(i, i ^ 1 << bit) for i in range(lax.axis_size(axis))])


def batch_weights(phase_rates, batch_rates, service_rates, source_rates, phase_rank, local_phases):
    phases = phase_rates.shape[0]
    moving = phase_rates * (1.0 - jnp.eye(phases, dtype=F32))
    leaving = jnp.sum(moving, axis=1) + jnp.sum(batch_rates, axis=(0, 2))
    sources_top = jnp.sum(jnp.maximum(source_rates[:, 2] + source_rates[:, 1], source_rates[:, 0]))
    uniform = jnp.max(leaving) + service_rates[0] + service_rates[1] + sources_top
    inverse = 1.0 / uniform
    start = phase_rank * local_phases
    tables = jnp.concatenate([moving[None], batch_rates], axis=0) * inverse
    tables = lax.dynamic_slice_in_dim(tables, start, local_phases, 2)
    tables = jnp.concatenate([tables, tables], axis=1)
    tables = lax.dynamic_slice_in_dim(tables, start, phases, 1)
    tables = jnp.swapaxes(tables, 1, 2)
    rounded = lax.reduce_precision(tables, 8, 7)
    high, low = rounded.astype(BF16), (tables - rounded).astype(BF16)
    weights = jnp.concatenate([high, low, high], axis=2).reshape(-1, 3 * phases)
    exits = lax.dynamic_slice_in_dim(leaving, start, local_phases, 0) * inverse
    exits = jnp.broadcast_to(exits[:, None], (local_phases, LANES))
    return weights, exits, inverse.reshape(1)


class Shape:
    def __init__(self, block, tiles, levels):
        self.slots, self.states, self.phases, self.wide_two, self.wide_one = block
        self.tiles = tiles
        self.levels = levels
        self.rows = self.slots * self.states * self.phases * self.wide_two
        self.rim_group = LANES // BATCH
        self.rim_parts = self.wide_two // self.rim_group
        self.rim_rows = self.states * self.rim_parts * self.phases
        self.edge_rows = self.slots * self.states * self.phases
        self.lane_step = 2 * max(self.wide_two, BATCH)
        self.per_small = LANES // self.lane_step
        self.small_rows = -(-self.states // self.per_small) * self.phases
        self.message_rows = self.edge_rows + self.small_rows

    def native(self, slot, state, u):
        start = (slot * self.states + state) * self.phases * self.wide_two + u
        return pl.ds(start, self.phases, stride=self.wide_two)

    def by_level(self, slot, state, u):
        start = ((slot * self.states + state) * self.wide_two + u) * self.phases
        if not isinstance(start, int):
            start = pl.multiple_of(start, self.phases)
        return pl.ds(start, self.phases)

    def small_at(self, state):
        return (state // self.per_small) * self.phases, (state % self.per_small) * self.lane_step


def lane_ids(shape):
    return lax.broadcasted_iota(jnp.int32, shape, len(shape) - 1)


def tile_at(owner, slot, tiles):
    found = jnp.int32(-1)
    for t in range(tiles):
        found = jnp.where(owner[t] == slot, t, found)
    return found


def route_of(routes, owner, tile, direction, slots):
    known = jnp.maximum(tile, 0)
    target = jnp.where(tile >= 0, routes[known, direction], -1)
    slot = owner[jnp.maximum(target, 0)]
    device = lax.div(slot, jnp.int32(slots))
    return target >= 0, device, slot - device * slots


def pack_edges(sh, me, routes, owner, at, data, rim_out, edge_out):
    n, phases = sh.levels, sh.phases
    lane = lane_ids((phases, LANES))
    first = tile_at(owner, me * sh.slots, sh.tiles)
    count = jnp.int32(0)
    for k in range(sh.slots):
        count = count + jnp.where(tile_at(owner, me * sh.slots + k, sh.tiles) >= 0, 1, 0)
    last_slot = count - 1
    rims = []
    bottoms = [jnp.zeros((phases, LANES), F32) for _ in range(sh.small_rows // phases)]
    for s in range(sh.states):
        row, base = sh.small_at(s)
        for part in range(sh.rim_parts):
            packed = jnp.zeros((phases, LANES), F32)
            for q in range(sh.rim_group):
                u = part * sh.rim_group + q
                block = data[at(last_slot, s, u), :]
                moved = pltpu.roll(block, (q * BATCH - (sh.wide_one - BATCH)) % LANES, 1)
                packed = jnp.where(lax.div(lane, jnp.int32(BATCH)) == q, moved, packed)
            rims.append(packed)
        for u in range(sh.wide_two):
            moved = pltpu.roll(data[at(0, s, u), :], base + u, 1)
            i = row // phases
            bottoms[i] = jnp.where(lane == base + u, moved, bottoms[i])
    for step in range(1, n):
        there = lax.rem(me + step, jnp.int32(n))
        their_first = tile_at(owner, there * sh.slots, sh.tiles)
        lower = first < their_first
        found, device, _ = route_of(routes, owner, their_first, 0, sh.slots)
        wanted = jnp.where(jnp.logical_and(found, device == me), 1.0, 0.0).astype(F32)
        for i, packed in enumerate(rims):
            rim_out[step - 1, i * phases:(i + 1) * phases, :] = packed * wanted
        small = list(bottoms)
        for k in range(sh.slots):
            tile = tile_at(owner, there * sh.slots + k, sh.tiles)
            _, _, left = route_of(routes, owner, tile, 2, sh.slots)
            _, _, right = route_of(routes, owner, tile, 3, sh.slots)
            _, _, corner = route_of(routes, owner, tile, 4, sh.slots)
            slot = jnp.where(lower, left, right)
            u = jnp.where(lower, sh.wide_two - 1, 0)
            for s in range(sh.states):
                start = (k * sh.states + s) * phases
                edge_out[step - 1, start:start + phases, :] = data[at(slot, s, u), :]
                row, base = sh.small_at(s)
                i = row // phases
                place = base + sh.lane_step // 2 + k
                moved = pltpu.roll(data[at(corner, s, sh.wide_two - 1), :], place, 1)
                small[i] = jnp.where(lane == place, moved, small[i])
        for i, values in enumerate(small):
            start = sh.edge_rows + i * phases
            edge_out[step - 1, start:start + phases, :] = values


def pack_kernel(sh, at, routes, owner, data, rim_out, edge_out):
    pack_edges(sh, lax.axis_index("level"), routes, owner, at, data, rim_out, edge_out)


def source_scalars(sources, scale, state, bits):
    feed = jnp.float32(0.0)
    outflow = jnp.float32(0.0)
    inflow = []
    for k in range(SOURCES):
        on = lax.rem(lax.shift_right_logical(state, jnp.int32(k)), jnp.int32(2)) == 1
        turn_on, turn_off, arrive = sources[k, 0], sources[k, 1], sources[k, 2]
        feed = feed + jnp.where(on, arrive, 0.0)
        outflow = outflow + jnp.where(on, turn_off, turn_on)
        inflow.append(jnp.where(on, turn_on, turn_off) * scale)
    return feed * scale, outflow * scale, inflow


def product_kernel(sh, bits, cross, first, deferred, *refs):
    refs = list(refs)
    levels_t, routes, owner, service, sources, scale_ref = refs[:6]
    weights, exits = refs[6:8]
    refs = refs[8:]
    n, phases, half = sh.levels, sh.phases, sh.lane_step // 2
    own = refs.pop(0)
    other = refs.pop(0)
    rim_own = refs.pop(0)
    rim_other = refs.pop(0)
    edges = [refs.pop(0) for _ in range(n - 1)]
    partners = [refs.pop(0) for _ in range(cross)]
    start_values = refs.pop(0) if deferred and not first else None
    out = refs.pop(0)
    if first:
        sent = refs.pop(0) if deferred else None
        rim_out, edge_out = refs.pop(0), refs.pop(0)
    at = sh.native if first else sh.by_level
    at_out = sh.by_level if first else sh.native
    me = lax.axis_index("level")
    src_rank = lax.axis_index("src")
    scale = scale_ref[0]
    serve_one, serve_two = service[0] * scale, service[1] * scale
    lane = lane_ids((phases, LANES))
    group_lane = lax.rem(lane, jnp.int32(BATCH))

    def split(values):
        high = values.astype(BF16)
        low = (values - high.astype(F32)).astype(BF16)
        return jnp.concatenate([high, high, low], axis=0)

    def slot_state(index, carry):
        k = lax.div(index, jnp.int32(sh.states))
        s = index - k * sh.states
        tile = tile_at(owner, me * sh.slots + k, sh.tiles)
        known = jnp.maximum(tile, 0)
        a, c = levels_t[known, 0], levels_t[known, 1]
        routed = [route_of(routes, owner, tile, r, sh.slots) for r in range(5)]

        def remote(which, rows):
            found, device, slot = routed[which]
            value = jnp.zeros((phases, LANES), F32)
            for step in range(1, n):
                source = lax.rem(me + n - step, jnp.int32(n))
                take = jnp.logical_and(found, device == source)
                value = jnp.where(take, edges[step - 1][rows, :], value)
            return value

        def is_local(which):
            found, device, _ = routed[which]
            return jnp.logical_and(found, device == me)

        def local_slot(which):
            return jnp.minimum(routed[which][2], sh.slots - 1)

        edge_at = pl.ds(pl.multiple_of((k * sh.states + s) * phases, phases), phases)
        small_row = lax.div(s, jnp.int32(sh.per_small)) * phases
        small_base = lax.rem(s, jnp.int32(sh.per_small)) * sh.lane_step
        small_at = pl.ds(pl.multiple_of(sh.edge_rows + small_row, phases), phases)
        left_row = jnp.where(is_local(2), own[at(local_slot(2), s, sh.wide_two - 1), :], remote(2, edge_at))
        right_row = jnp.where(is_local(3), own[at(local_slot(3), s, 0), :], remote(3, edge_at))
        above_small = remote(1, small_at)
        above_local = is_local(1)
        corner_small = pltpu.roll(remote(4, small_at), LANES - (small_base + half + k), 1)
        corner = jnp.where(is_local(4), own[at(local_slot(4), s, sh.wide_two - 1), :], corner_small)

        state = src_rank * sh.states + s
        feed, outflow, inflow = source_scalars(sources, scale, state, bits)
        base_diag = 1.0 - feed - outflow
        diagonal = base_diag - exits[...]
        diagonal = diagonal - jnp.where(jnp.logical_or(lane > 0, a > 0), serve_one, 0.0)

        below_local = jnp.where(is_local(0), 1.0, 0.0).astype(F32)
        below_remote = jnp.where(jnp.logical_and(routed[0][0], jnp.logical_not(is_local(0))), 1.0, 0.0).astype(F32)
        rim_values = []
        for part in range(sh.rim_parts):
            halves = []
            start = pl.multiple_of((s * sh.rim_parts + part) * phases, phases)
            for values, received in ((own, rim_own), (other, rim_other)):
                packed = jnp.zeros((phases, LANES), F32)
                for q in range(sh.rim_group):
                    u = part * sh.rim_group + q
                    block = values[at(local_slot(0), s, u), :]
                    moved = pltpu.roll(block, (q * BATCH - (sh.wide_one - BATCH)) % LANES, 1)
                    packed = jnp.where(lax.div(lane, jnp.int32(BATCH)) == q, moved, packed)
                halves.append(packed * below_local + received[pl.ds(start, phases), :] * below_remote)
            product = jnp.dot(weights[...], split(jnp.concatenate(halves, axis=0)), preferred_element_type=F32)
            total = jnp.zeros((phases, LANES), F32)
            for b in range(1, BATCH + 1):
                moved = pltpu.roll(product[b * phases:(b + 1) * phases], (b - BATCH) % LANES, 1)
                total = total + jnp.where(group_lane < b, moved, 0.0)
            rim_values.append(total)

        if deferred:
            other_state = lax.bitwise_xor(state, jnp.int32(1 << bits))
            feed_there, outflow_there, _ = source_scalars(sources, scale, other_state, bits)
            feed_more = feed_there - feed
            diag_more = (feed + outflow) - (feed_there + outflow_there)
            if not first:
                there = source_scalars(sources, scale, other_state, bits)[2][bits]
                square = inflow[bits] * there

        for pair in range(sh.wide_two // 2):
            columns = []
            for u in (2 * pair, 2 * pair + 1):
                columns.append(split(jnp.concatenate([own[at(k, s, u), :], other[at(k, s, u), :]], axis=0)))
            product = jnp.dot(weights[...], jnp.concatenate(columns, axis=1), preferred_element_type=F32)
            for j, u in enumerate((2 * pair, 2 * pair + 1)):
                lanes = slice(j * LANES, (j + 1) * LANES)
                part, q = u // sh.rim_group, u % sh.rim_group
                total = product[0:phases, lanes]
                for b in range(1, BATCH + 1):
                    moved = pltpu.roll(product[b * phases:(b + 1) * phases, lanes], b, 1)
                    total = total + jnp.where(lane >= b, moved, 0.0)
                rim = rim_values[part]
                if q:
                    rim = pltpu.roll(rim, LANES - q * BATCH, 1)
                total = total + jnp.where(lane < BATCH, rim, 0.0)
                here = own[at(k, s, u), :]
                if u:
                    before = own[at(k, s, u - 1), :]
                    beyond = jnp.where(
                        above_local,
                        own[at(local_slot(1), s, u - 1), :],
                        pltpu.roll(above_small, LANES - (small_base + u - 1), 1),
                    )
                else:
                    before, beyond = left_row, corner
                after = own[at(k, s, u + 1), :] if u + 1 < sh.wide_two else right_row
                shifted = pltpu.roll(jnp.where(lane == 0, beyond, before), LANES - 1, 1)
                two = jnp.where(jnp.logical_or(u > 0, c > 0), serve_two, 0.0)
                total = total + (diagonal - two) * here
                total = total + serve_one * shifted + serve_two * after + feed * before
                for bit in range(bits):
                    flipped = lax.bitwise_xor(s, jnp.int32(1 << bit))
                    total = total + inflow[bit] * own[at(k, flipped, u), :]
                for bit, values in enumerate(partners):
                    total = total + inflow[bits + bit] * values[at(k, s, u), :]
                if deferred and not first:
                    total = total + square * start_values[sh.native(k, s, u), :]
                if not first:
                    total = jnp.where(tile >= 0, total, 0.0)
                out[at_out(k, s, u), :] = total
                if deferred and first:
                    sent[sh.native(k, s, u), :] = 2.0 * total + feed_more * before + diag_more * here
        return carry

    lax.fori_loop(0, sh.slots * sh.states, slot_state, 0)
    if first:
        pack_edges(sh, me, routes, owner, sh.by_level, out, rim_out, edge_out)


def join_kernel(sh, bits, owner, sources, scale_ref, stepped, received, out):
    me = lax.axis_index("level")
    src_rank = lax.axis_index("src")
    k = pl.program_id(0)
    filled = tile_at(owner, me * sh.slots + k, sh.tiles) >= 0
    inflow = source_scalars(sources, scale_ref[0], src_rank * sh.states, bits)[2][bits]
    out[...] = jnp.where(filled, stepped[...] + inflow * received[...], 0.0)


def body(
    state_values,
    phase_rates,
    batch_rates,
    service_rates,
    source_rates,
    tile_levels,
    routes,
    tile_owner,
):
    block = state_values.shape
    sh = Shape(block, tile_owner.shape[0], lax.axis_size("level"))
    bits = sh.states.bit_length() - 1
    cross = SOURCES - bits
    deferred = cross == 1
    n = sh.levels
    flat = state_values.reshape(sh.rows, LANES)
    weights, exits, scale = batch_weights(
        phase_rates, batch_rates, service_rates, source_rates, lax.axis_index("phase"), sh.phases
    )
    smem, vmem = pl.BlockSpec(memory_space=SM), pl.BlockSpec(memory_space=VM)
    rows_shape = jax.ShapeDtypeStruct((sh.rows, LANES), F32)
    edge_shapes = (
        jax.ShapeDtypeStruct((n - 1, sh.rim_rows, LANES), F32),
        jax.ShapeDtypeStruct((n - 1, sh.message_rows, LANES), F32),
    )
    rims, edges = pl.pallas_call(
        functools.partial(pack_kernel, sh, sh.native),
        out_shape=edge_shapes,
        in_specs=[smem, smem, vmem],
        out_specs=(vmem, vmem),
    )(routes, tile_owner, flat)

    def exchange(values, rims, edges):
        other = shift_from(values, "phase", 1)
        rim_got = sum(shift_from(rims[i], "level", -(i + 1)) for i in range(n - 1))
        rim_other = shift_from(rim_got, "phase", 1)
        edge_got = [shift_from(edges[i], "level", -(i + 1)) for i in range(n - 1)]
        return [values, other, rim_got, rim_other] + edge_got

    def product(first, inputs, extra):
        operands = [tile_levels, routes, tile_owner, service_rates, source_rates, scale, weights, exits] + inputs + extra
        shapes = [rows_shape]
        if first:
            shapes += ([rows_shape] if deferred else []) + list(edge_shapes)
        return pl.pallas_call(
            functools.partial(product_kernel, sh, bits, 0 if deferred else cross, first, deferred),
            out_shape=tuple(shapes),
            in_specs=[smem] * 6 + [vmem] * (len(operands) - 6),
            out_specs=tuple([vmem] * len(shapes)),
        )(*operands)

    extra = [] if deferred else [from_partner(flat, "src", bit) for bit in range(cross)]
    outs = product(True, exchange(flat, rims, edges), extra)
    if deferred:
        once, sent, rims, edges = outs
        received = from_partner(sent, "src", 0)
        (twice,) = product(False, exchange(once, rims, edges), [flat])
        tile_spec = pl.BlockSpec((sh.rows // sh.slots, LANES), lambda k: (k, 0))
        result = pl.pallas_call(
            functools.partial(join_kernel, sh, bits),
            grid=(sh.slots,),
            out_shape=rows_shape,
            in_specs=[smem, smem, smem, tile_spec, tile_spec],
            out_specs=tile_spec,
        )(tile_owner, source_rates, scale, twice, received)
    else:
        once, rims, edges = outs
        extra = [from_partner(once, "src", bit) for bit in range(cross)]
        (result,) = product(False, exchange(once, rims, edges), extra)
    return result.reshape(block)


def solution(mesh):
    placed = (
        P(("groups", "level"), "src", "phase", None, None),
        P("groups", None),
        P("groups", None, None),
        P("groups"),
        P("groups", None),
        P("groups", None),
        P("groups", None),
        P("groups"),
    )
    return jax.shard_map(
        body,
        mesh=mesh,
        in_specs=placed,
        out_specs=P(("groups", "level"), "src", "phase", None, None),
        check_vma=False,
    )
```

```python
import functools

import jax
import jax.numpy as jnp
from jax import lax
from jax.experimental import pallas as pl
from jax.experimental.pallas import tpu as pltpu
from jax.sharding import PartitionSpec as P

BATCH = 16
SOURCES = 3
LANES = 128
F32 = jnp.float32
BF16 = jnp.bfloat16
I32 = jnp.int32
VM = pltpu.VMEM
SM = pltpu.SMEM
GRANT = 24 << 20

FEED, STAY, FEED_MORE, STAY_MORE, SQUARE, INFLOW = 0, 1, 2, 3, 4, 5
TILE, LEVEL_ONE, LEVEL_TWO, ROUTES = 0, 1, 2, 3
BELOW, ABOVE, LEFT, RIGHT, CORNER = 0, 1, 2, 3, 4
ROW, WANTED, LAST, PICKS = 0, 1, 2, 3


def permute(x, axis, pairs_of):
    return lax.ppermute(x, axis, [(i, pairs_of(i)) for i in range(lax.axis_size(axis))])


def from_next(x, axis):
    n = lax.axis_size(axis)
    return permute(x, axis, lambda i: (i - 1) % n)


def from_partner(x, axis, bit):
    return permute(x, axis, lambda i: i ^ 1 << bit)


class Shape:
    def __init__(self, block, tiles, levels):
        self.slots, self.states, self.phases, self.wide_two, self.wide_one = block
        self.tiles = tiles
        self.levels = levels
        self.units = self.slots * self.states
        self.rows = self.units * self.phases * self.wide_two
        self.rim_group = LANES // BATCH
        self.rim_parts = self.wide_two // self.rim_group
        self.state_rim_rows = self.states * self.rim_parts * self.phases
        self.rim_rows = self.slots * self.state_rim_rows
        self.edge_rows = self.units * self.phases
        self.lane_step = 2 * max(self.wide_two, BATCH)
        self.per_small = LANES // self.lane_step
        self.small_blocks = -(-self.states // self.per_small)
        self.small_rows_at = self.state_rim_rows + self.edge_rows
        self.message_rows = self.small_rows_at + self.small_blocks * self.phases
        self.bits = self.states.bit_length() - 1
        self.cross = SOURCES - self.bits
        self.deferred = self.cross == 1
        self.raw_end = self.states
        self.mid_end = self.units - self.states
        self.raw_rows = self.raw_end * self.wide_two * self.phases
        self.mid_rows = (self.mid_end - self.raw_end) * self.wide_two * self.phases
        self.ends_at = self.states * self.wide_two * self.phases
        self.rims_at = self.ends_at + self.mid_end * 2 * self.phases
        self.columns_at = self.rims_at + self.mid_end * self.rim_parts * self.phases
        self.per_column = LANES // self.wide_two
        self.late_rows = self.columns_at + -(-self.mid_end // self.per_column) * self.phases
        self.power = levels & (levels - 1) == 0

    def at(self, start):
        if not isinstance(start, int):
            start = pl.multiple_of(start, self.phases)
        return pl.ds(start, self.phases)

    def native(self, unit, u):
        return pl.ds(unit * self.phases * self.wide_two + u, self.phases, stride=self.wide_two)

    def by_level(self, unit, u):
        return self.at((unit * self.wide_two + u) * self.phases)

    def rim_at(self, unit, part):
        return self.at((unit * self.rim_parts + part) * self.phases)

    def small_at(self, state):
        return state // self.per_small, (state % self.per_small) * self.lane_step

    def sends_to(self, me, step):
        return me ^ step if self.power else (me + step) % self.levels

    def takes_from(self, me, step):
        return me ^ step if self.power else (me + self.levels - step) % self.levels


def lane_ids(shape):
    return lax.broadcasted_iota(I32, shape, len(shape) - 1)


def tile_at(owner, slot, tiles):
    found = jnp.int32(-1)
    for t in range(tiles):
        found = jnp.where(owner[t] == slot, t, found)
    return found


def route_of(routes, owner, tile, direction, slots):
    known = jnp.maximum(tile, 0)
    target = jnp.where(tile >= 0, routes[known, direction], -1)
    slot = owner[jnp.maximum(target, 0)]
    device = lax.div(slot, jnp.int32(slots))
    return target >= 0, device, slot - device * slots


def peer(sh, me, step, sending):
    if sh.power:
        return lax.bitwise_xor(me, jnp.int32(step))
    return lax.rem(me + (step if sending else sh.levels - step), jnp.int32(sh.levels))


def fill_send_plan(sh, routes, owner, plan):
    me = lax.axis_index("level")
    first = tile_at(owner, me * sh.slots, sh.tiles)
    count = jnp.int32(0)
    for k in range(sh.slots):
        count = count + jnp.where(tile_at(owner, me * sh.slots + k, sh.tiles) >= 0, 1, 0)
    for step in range(1, sh.levels):
        there = peer(sh, me, step, True)
        their_first = tile_at(owner, there * sh.slots, sh.tiles)
        lower = first < their_first
        found, device, _ = route_of(routes, owner, their_first, BELOW, sh.slots)
        plan[step - 1, ROW] = jnp.where(lower, sh.wide_two - 1, 0)
        plan[step - 1, WANTED] = jnp.where(jnp.logical_and(found, device == me), 1, 0)
        plan[step - 1, LAST] = (count - 1) * sh.states
        for k in range(sh.slots):
            tile = tile_at(owner, there * sh.slots + k, sh.tiles)
            _, _, left = route_of(routes, owner, tile, LEFT, sh.slots)
            _, _, right = route_of(routes, owner, tile, RIGHT, sh.slots)
            _, _, corner = route_of(routes, owner, tile, CORNER, sh.slots)
            plan[step - 1, PICKS + 2 * k] = jnp.where(lower, left, right) * sh.states
            plan[step - 1, PICKS + 2 * k + 1] = corner * sh.states


def add_packed(sh, lane, rims, column, u, values):
    part, q = u // sh.rim_group, u % sh.rim_group
    moved = pltpu.roll(values, (q * BATCH - (sh.wide_one - BATCH)) % LANES, 1)
    rims[part] = jnp.where(lax.div(lane, jnp.int32(BATCH)) == q, moved, rims[part])
    moved = pltpu.roll(values, u, 1) if u else values
    return jnp.where(lane == u, moved, column)


def write_messages(sh, plan, data, rims, columns, messages):
    phases, last_u = sh.phases, sh.wide_two - 1
    lane = lane_ids((phases, LANES))
    bottoms = [jnp.zeros((phases, LANES), F32) for _ in range(sh.small_blocks)]
    for s in range(sh.states):
        block, base = sh.small_at(s)
        values = columns[sh.at(s * phases), :]
        bottoms[block] = bottoms[block] + (pltpu.roll(values, base, 1) if base else values)
    for step in range(1, sh.levels):
        row = plan[step - 1, ROW]
        wanted = jnp.where(plan[step - 1, WANTED] > 0, 1.0, 0.0).astype(F32)
        last = plan[step - 1, LAST]
        for s in range(sh.states):
            for part in range(sh.rim_parts):
                messages[step - 1][sh.rim_at(s, part), :] = rims[sh.rim_at(last + s, part), :] * wanted
        small = list(bottoms)
        for k in range(sh.slots):
            slot, corner = plan[step - 1, PICKS + 2 * k], plan[step - 1, PICKS + 2 * k + 1]
            for s in range(sh.states):
                messages[step - 1][sh.at(sh.state_rim_rows + (k * sh.states + s) * phases), :] = data[sh.by_level(slot + s, row), :]
                block, base = sh.small_at(s)
                place = base + sh.lane_step // 2 + k
                moved = pltpu.roll(columns[sh.at((corner + s) * phases), :], (place - last_u) % LANES, 1)
                small[block] = jnp.where(lane == place, moved, small[block])
        for i, values in enumerate(small):
            messages[step - 1][sh.at(sh.small_rows_at + i * phases), :] = values


def pack_kernel(sh, routes, owner, data, send_plan, *outs):
    raw, (by_level, rims, columns, *messages) = (outs[0], outs[1:]) if sh.deferred else (None, outs)
    lane = lane_ids((sh.phases, LANES))
    fill_send_plan(sh, routes, owner, send_plan)

    def reorder(to_src, unit, carry):
        packed = [jnp.zeros((sh.phases, LANES), F32) for _ in range(sh.rim_parts)]
        column = jnp.zeros((sh.phases, LANES), F32)
        for u in range(sh.wide_two):
            values = data[sh.native(unit, u), :]
            by_level[sh.by_level(unit, u), :] = values
            if to_src:
                raw[sh.by_level(unit, u), :] = values
            column = add_packed(sh, lane, packed, column, u, values)
        for part, values in enumerate(packed):
            rims[sh.rim_at(unit, part), :] = values
        columns[sh.at(unit * sh.phases), :] = column
        return carry

    first = sh.raw_end if sh.deferred else 0
    if sh.deferred:
        lax.fori_loop(0, first, functools.partial(reorder, True), 0)
    lax.fori_loop(first, sh.units, functools.partial(reorder, False), 0)
    write_messages(sh, send_plan, by_level, rims, columns, messages)


def source_scalars(sources, scale, state):
    feed = jnp.float32(0.0)
    outflow = jnp.float32(0.0)
    inflow = []
    for k in range(SOURCES):
        on = lax.rem(lax.shift_right_logical(state, jnp.int32(k)), jnp.int32(2)) == 1
        turn_on, turn_off, arrive = sources[k, 0], sources[k, 1], sources[k, 2]
        feed = feed + jnp.where(on, arrive, 0.0)
        outflow = outflow + jnp.where(on, turn_off, turn_on)
        inflow.append(jnp.where(on, turn_on, turn_off) * scale)
    return feed * scale, outflow * scale, inflow


def prep_kernel(sh, routes, owner, levels_t, service, sources, phase_rates, batch_rates, plan, rates, paired, single,
                exits, turned, wide):
    me = lax.axis_index("level")
    for k in range(sh.slots):
        tile = tile_at(owner, me * sh.slots + k, sh.tiles)
        known = jnp.maximum(tile, 0)
        plan[k, TILE] = tile
        plan[k, LEVEL_ONE] = levels_t[known, 0]
        plan[k, LEVEL_TWO] = levels_t[known, 1]
        for r in range(5):
            found, device, slot = route_of(routes, owner, tile, r, sh.slots)
            kind = jnp.int32(1)
            for step in range(1, sh.levels):
                kind = jnp.where(device == peer(sh, me, step, False), step + 1, kind)
            plan[k, ROUTES + 3 * r] = jnp.where(found, kind, 0)
            plan[k, ROUTES + 3 * r + 1] = slot * sh.states
            plan[k, ROUTES + 3 * r + 2] = jnp.where(slot == 0, 1, 0)

    phases, full = sh.phases, phase_rates.shape[0]
    start = lax.axis_index("phase") * phases
    rows_here = pl.ds(pl.multiple_of(start, phases), phases)
    shape = (full, full)
    moving = phase_rates[...]
    moving = jnp.where(lax.broadcasted_iota(I32, shape, 0) == lax.broadcasted_iota(I32, shape, 1), 0.0, moving)
    total = moving
    for b in range(BATCH):
        total = total + batch_rates[b]
    leaving = jnp.sum(total, axis=1, keepdims=True)
    sources_top = jnp.float32(0.0)
    for k in range(SOURCES):
        sources_top = sources_top + jnp.maximum(sources[k, 2] + sources[k, 1], sources[k, 0])
    uniform = jnp.max(leaving) + (service[0] + service[1] + sources_top)
    inverse = 1.0 / jnp.full((phases, LANES), uniform, F32)
    scale = jnp.max(inverse)
    wide[...] = jnp.broadcast_to(leaving, (full, LANES))
    exits[...] = wide[rows_here, :] * inverse

    base = lax.axis_index("src") * sh.states
    rates[sh.states, 0] = service[0] * scale
    rates[sh.states, 1] = service[1] * scale
    for s in range(sh.states):
        state = base + s
        feed, outflow, inflow = source_scalars(sources, scale, state)
        rates[s, FEED] = feed
        rates[s, STAY] = 1.0 - feed - outflow
        for k in range(SOURCES):
            rates[s, INFLOW + k] = inflow[k]
        if sh.deferred:
            there = lax.bitwise_xor(state, jnp.int32(1 << sh.bits))
            feed_there, outflow_there, inflow_there = source_scalars(sources, scale, there)
            rates[s, FEED_MORE] = feed_there - feed
            rates[s, STAY_MORE] = (feed + outflow) - (feed_there + outflow_there)
            rates[s, SQUARE] = inflow[sh.bits] * inflow_there[sh.bits]

    for b in range(BATCH + 2):
        if b <= BATCH:
            values = (moving if b == 0 else batch_rates[b - 1]) * scale
            turned[0:full, :] = values
            turned[full:2 * full, :] = values
            turned[0:full, :] = turned[pl.ds(pl.multiple_of(start, phases), full), :].T
            values = turned[rows_here, :]
            high = values.astype(BF16)
            low = (values - high.astype(F32)).astype(BF16)
        else:
            high = jnp.zeros((phases, full), BF16)
            low = high
        parts = (high, low, high)
        for i, part in enumerate(parts):
            if 1 <= b <= BATCH:
                single[(b - 1) * phases:b * phases, i * full:(i + 1) * full] = part
            column = (b % 2) * 3 * full + i * full
            paired[(b // 2) * phases:(b // 2 + 1) * phases, column:column + full] = part


def split(values):
    high = values.astype(BF16)
    low = (values - high.astype(F32)).astype(BF16)
    return [high, high, low]


def inner_kernel(sh, first, plan, rates, weights, exits, own, other, *outs):
    phases = sh.phases
    out = outs[0]
    sent = outs[1] if first and sh.deferred else None
    other_at = sh.native if first else sh.by_level
    serve_one, serve_two = rates[sh.states, 0], rates[sh.states, 1]
    lane = lane_ids((phases, LANES))

    def unit_step(sending, unit, carry):
        k = lax.div(unit, jnp.int32(sh.states))
        s = unit - k * sh.states
        a, c = plan[k, LEVEL_ONE], plan[k, LEVEL_TWO]
        feed = rates[s, FEED]
        stay = rates[s, STAY] - exits[...] - jnp.where(jnp.logical_or(lane > 0, a > 0), serve_one, 0.0)
        for pair in range(sh.wide_two // 2):
            columns = []
            for u in (2 * pair, 2 * pair + 1):
                values = jnp.concatenate([own[sh.by_level(unit, u), :], other[other_at(unit, u), :]], axis=0)
                columns.append(jnp.concatenate(split(values) + split(pltpu.roll(values, 1, 1)), axis=0))
            product = jnp.dot(weights[...], jnp.concatenate(columns, axis=1), preferred_element_type=F32)
            for j, u in enumerate((2 * pair, 2 * pair + 1)):
                lanes = slice(j * LANES, (j + 1) * LANES)
                total = product[0:phases, lanes]
                for b in range(1, BATCH // 2 + 1):
                    total = total + pltpu.roll(product[b * phases:(b + 1) * phases, lanes], 2 * b, 1)
                here = own[sh.by_level(unit, u), :]
                two = serve_two if u else jnp.where(c > 0, serve_two, 0.0)
                total = total + (stay - two) * here
                if u:
                    prev = own[sh.by_level(unit, u - 1), :]
                    total = total + serve_one * pltpu.roll(prev, LANES - 1, 1) + feed * prev
                if u + 1 < sh.wide_two:
                    total = total + serve_two * own[sh.by_level(unit, u + 1), :]
                for bit in range(sh.bits):
                    flipped = unit - s + lax.bitwise_xor(s, jnp.int32(1 << bit))
                    total = total + rates[s, INFLOW + bit] * own[sh.by_level(flipped, u), :]
                out[sh.by_level(unit, u), :] = total
                if sending:
                    more = rates[s, STAY_MORE] * here
                    if u:
                        more = more + rates[s, FEED_MORE] * prev
                    sent[sh.by_level(unit - sh.raw_end, u), :] = 2.0 * total + more
        return carry

    if sent is not None:
        lax.fori_loop(sh.raw_end, sh.mid_end, functools.partial(unit_step, True), 0)
        lax.fori_loop(0, sh.raw_end, functools.partial(unit_step, False), 0)
        lax.fori_loop(sh.mid_end, sh.units, functools.partial(unit_step, False), 0)
    else:
        lax.fori_loop(0, sh.units, functools.partial(unit_step, False), 0)


def halo_kernel(sh, first, *refs):
    refs = list(refs)
    n, phases, last_u = sh.levels, sh.phases, sh.wide_two - 1
    plan, rates = refs[:2]
    refs = refs[2:]
    send_plan = refs.pop(0) if first else None
    weights, inner, own, rims_own, rims_other, columns_own, rim_got, rim_other = refs[:8]
    refs = refs[8:]
    edges, refs = refs[:n - 1], refs[n - 1:]
    raw = 0 if sh.deferred else sh.cross
    partners, refs = refs[:raw], refs[raw:]
    raw_got = refs.pop(0) if sh.deferred else None
    start_values = refs.pop(0) if sh.deferred and not first else None
    out = refs.pop(0)
    sent = refs.pop(0) if sh.deferred and first else None
    rims_out, columns_out = (refs.pop(0), refs.pop(0)) if first else (None, None)
    serve_one, serve_two = rates[sh.states, 0], rates[sh.states, 1]
    lane = lane_ids((phases, LANES))
    group_lane = lax.rem(lane, jnp.int32(BATCH))
    zero = jnp.zeros((phases, LANES), F32)
    if sent is not None:
        for start in range(sh.columns_at, sh.late_rows, phases):
            sent[start:start + phases, :] = zero

    def rim_product(halves):
        columns = [jnp.concatenate(split(jnp.concatenate(pair, axis=0)), axis=0) for pair in halves]
        product = jnp.dot(weights[...], jnp.concatenate(columns, axis=1), preferred_element_type=F32)
        sums = []
        for i in range(len(halves)):
            total = zero
            for b in range(1, BATCH + 1):
                block = product[(b - 1) * phases:b * phases, i * LANES:(i + 1) * LANES]
                total = total + jnp.where(group_lane < b, pltpu.roll(block, (b - BATCH) % LANES, 1), 0.0)
            sums.append(total)
        return sums

    def unit_step(group, unit, carry):
        k = lax.div(unit, jnp.int32(sh.states))
        s = unit - k * sh.states

        def kind(which):
            return plan[k, ROUTES + 3 * which]

        def beside(which):
            return plan[k, ROUTES + 3 * which + 1] + s

        def kept(which):
            return jnp.where(plan[k, ROUTES + 3 * which + 2] > 0, 0.0, 1.0).astype(F32)

        def number(flag):
            return jnp.where(flag, 1.0, 0.0).astype(F32)

        def remote(which, rows):
            value = zero
            for step in range(1, n):
                value = jnp.where(kind(which) == step + 1, edges[step - 1][rows, :], value)
            return value

        small_base = lax.rem(s, jnp.int32(sh.per_small)) * sh.lane_step
        small_at = sh.at(sh.small_rows_at + lax.div(s, jnp.int32(sh.per_small)) * phases)
        edge_at = sh.at(sh.state_rim_rows + unit * phases)
        left = jnp.where(kind(LEFT) == 1, own[sh.by_level(beside(LEFT), last_u), :], remote(LEFT, edge_at))
        right = jnp.where(kind(RIGHT) == 1, own[sh.by_level(beside(RIGHT), 0), :], remote(RIGHT, edge_at))
        above = jnp.where(
            kind(ABOVE) == 1,
            columns_own[sh.at(beside(ABOVE) * phases), :],
            pltpu.roll(remote(ABOVE, small_at), LANES - small_base, 1),
        )
        above = jnp.where(lane < sh.wide_two, above, 0.0) * serve_one
        corner = jnp.where(
            kind(CORNER) == 1,
            pltpu.roll(columns_own[sh.at(beside(CORNER) * phases), :], LANES - 1 - last_u, 1),
            pltpu.roll(remote(CORNER, small_at), LANES - 1 - (small_base + sh.lane_step // 2 + k), 1),
        )
        corner = jnp.where(lane == LANES - 1, corner, 0.0) * serve_one
        shifted = jnp.where(lane == LANES - 1, 0.0, pltpu.roll(left, LANES - 1, 1)) * serve_one
        own_column = columns_own[sh.at(unit * phases), :] * serve_one
        below_local, below_remote = number(kind(BELOW) == 1), number(kind(BELOW) > 1)
        under, mine = [], []
        for part in range(sh.rim_parts):
            under.append([
                rims_own[sh.rim_at(beside(BELOW), part), :] * below_local + rim_got[sh.rim_at(s, part), :] * below_remote,
                rims_other[sh.rim_at(beside(BELOW), part), :] * below_local
                + rim_other[sh.rim_at(s, part), :] * below_remote,
            ])
            mine.append([rims_own[sh.rim_at(unit, part), :], rims_other[sh.rim_at(unit, part), :]])
        feed = rates[s, FEED]
        if group is None:
            rims = rim_product([[p - q for p, q in zip(*both)] for both in zip(under, mine)])
        else:
            sums = rim_product(under + mine)
            reach, wrap = sums[:sh.rim_parts], sums[sh.rim_parts:]
            rims = [p - q for p, q in zip(reach, wrap)]
            drop = jnp.float32(0.0 if group == "raw" else 1.0)
            keep_left = kept(LEFT)
            sent_rims = [2.0 * (kept(BELOW) * p - drop * q) for p, q in zip(reach, wrap)]
            sent_column = 2.0 * (kept(ABOVE) * above - drop * own_column)
            sent_first = (2.0 * keep_left) * (shifted + feed * left) + (2.0 * kept(CORNER)) * corner
            sent_first = sent_first + ((2.0 * keep_left - 1.0) * rates[s, FEED_MORE]) * left
            sent_last = (2.0 * kept(RIGHT) * serve_two) * right
            if group != "last":
                sent[sh.at(sh.ends_at + 2 * unit * phases), :] = sent_first
                sent[sh.at(sh.ends_at + (2 * unit + 1) * phases), :] = sent_last
                for part in range(sh.rim_parts):
                    sent[sh.at(sh.rims_at + (unit * sh.rim_parts + part) * phases), :] = sent_rims[part]
                place = sh.at(sh.columns_at + lax.div(unit, jnp.int32(sh.per_column)) * phases)
                base = lax.rem(unit, jnp.int32(sh.per_column)) * sh.wide_two
                sent[place, :] = sent[place, :] + pltpu.roll(sent_column, base, 1)
        column = above - own_column
        packed, packed_column = [zero] * sh.rim_parts, zero
        for u in range(sh.wide_two):
            part, q = u // sh.rim_group, u % sh.rim_group

            def unpacked(rims, column):
                value = jnp.where(lane < BATCH, pltpu.roll(rims[part], LANES - q * BATCH, 1) if q else rims[part], 0.0)
                if u:
                    value = jnp.where(lane == LANES - 1, pltpu.roll(column, LANES - u, 1), value)
                return value

            inside = inner[sh.by_level(unit, u), :]
            total = inside + unpacked(rims, column)
            if u == 0:
                total = total + shifted + corner + feed * left
            if u == last_u:
                total = total + serve_two * right
            for bit, values in enumerate(partners):
                total = total + rates[s, INFLOW + sh.bits + bit] * values[sh.by_level(unit, u), :]
            if group == "raw":
                total = total + (2.0 * rates[s, INFLOW + sh.bits]) * raw_got[sh.by_level(unit, u), :]
            if start_values is not None:
                total = total + rates[s, SQUARE] * start_values[sh.by_level(unit, u), :]
            if raw_got is not None and carry == "raw":
                more = rates[s, STAY_MORE] * raw_got[sh.by_level(unit, u), :]
                if u:
                    more = more + rates[s, FEED_MORE] * raw_got[sh.by_level(unit, u - 1), :]
                total = total + rates[s, INFLOW + sh.bits] * more
            if first:
                packed_column = add_packed(sh, lane, packed, packed_column, u, total)
            if first or sh.deferred:
                out[sh.by_level(unit, u), :] = total
            else:
                out[sh.native(unit, u), :] = jnp.where(plan[k, TILE] >= 0, total, 0.0)
            if group == "last":
                value = 2.0 * inside + unpacked(sent_rims, sent_column) + rates[s, STAY_MORE] * own[sh.by_level(unit, u), :]
                if u:
                    value = value + rates[s, FEED_MORE] * own[sh.by_level(unit, u - 1), :]
                else:
                    value = value + sent_first
                if u == last_u:
                    value = value + sent_last
                sent[sh.by_level(unit - sh.mid_end, u), :] = value
        if first:
            for part in range(sh.rim_parts):
                rims_out[sh.rim_at(unit, part), :] = packed[part]
            columns_out[sh.at(unit * phases), :] = packed_column

    def sweep(start, stop, group, mark=None):
        def step(unit, carry):
            unit_step(group, unit, mark)
            return carry

        lax.fori_loop(start, stop, step, 0)

    if sent is not None:
        sweep(0, sh.raw_end, "raw")
        sweep(sh.raw_end, sh.mid_end, "mid")
        sweep(sh.mid_end, sh.units, "last")
    elif sh.deferred:
        sweep(0, sh.raw_end, None, "raw")
        sweep(sh.raw_end, sh.units, None)
    else:
        sweep(0, sh.units, None)
    if first:
        write_messages(sh, send_plan, out, rims_out, columns_out, refs)


def join_kernel(sh, plan, rates, stepped, got_mid, got_late, out):
    phases, last_u = sh.phases, sh.wide_two - 1
    lane = lane_ids((phases, LANES))
    inflow = rates[0, INFLOW + sh.bits]

    def unit_step(group, unit, carry):
        filled = plan[lax.div(unit, jnp.int32(sh.states)), TILE] >= 0
        if group != "last":
            rims = [
                got_late[sh.at(sh.rims_at + (unit * sh.rim_parts + part) * phases), :] for part in range(sh.rim_parts)
            ]
            column = got_late[sh.at(sh.columns_at + lax.div(unit, jnp.int32(sh.per_column)) * phases), :]
            base = lax.rem(unit, jnp.int32(sh.per_column)) * sh.wide_two
        for u in range(sh.wide_two):
            if group == "last":
                got = got_late[sh.by_level(unit - sh.mid_end, u), :]
            else:
                part, q = u // sh.rim_group, u % sh.rim_group
                got = jnp.where(lane < BATCH, pltpu.roll(rims[part], LANES - q * BATCH, 1) if q else rims[part], 0.0)
                if u:
                    got = jnp.where(lane == LANES - 1, pltpu.roll(column, LANES - (base + u), 1), got)
                if u in (0, last_u):
                    got = got + got_late[sh.at(sh.ends_at + (2 * unit + (1 if u else 0)) * phases), :]
                if group == "mid":
                    got = got + got_mid[sh.by_level(unit - sh.raw_end, u), :]
            total = stepped[sh.by_level(unit, u), :] + inflow * got
            out[sh.native(unit, u), :] = jnp.where(filled, total, 0.0)
        return carry

    lax.fori_loop(0, sh.raw_end, functools.partial(unit_step, "raw"), 0)
    lax.fori_loop(sh.raw_end, sh.mid_end, functools.partial(unit_step, "mid"), 0)
    lax.fori_loop(sh.mid_end, sh.units, functools.partial(unit_step, "last"), 0)


def body(
    state_values,
    phase_rates,
    batch_rates,
    service_rates,
    source_rates,
    tile_levels,
    routes,
    tile_owner,
):
    block = state_values.shape
    sh = Shape(block, tile_owner.shape[0], lax.axis_size("level"))
    n, full = sh.levels, phase_rates.shape[0]
    flat = state_values.reshape(sh.rows, LANES)
    smem, vmem = pl.BlockSpec(memory_space=SM), pl.BlockSpec(memory_space=VM)

    def array(rows):
        return jax.ShapeDtypeStruct((rows, LANES), F32)

    def table(rows, columns, dtype=F32):
        return jax.ShapeDtypeStruct((rows, columns), dtype)

    def call(kernel, scalars, arrays, shapes, micros, scalar_shapes=(), scratch=()):
        return pl.pallas_call(
            kernel,
            out_shape=tuple(scalar_shapes) + tuple(shapes),
            in_specs=[smem] * len(scalars) + [vmem] * len(arrays),
            out_specs=tuple([smem] * len(scalar_shapes) + [vmem] * len(shapes)),
            scratch_shapes=list(scratch),
            cost_estimate=pl.CostEstimate(flops=0, bytes_accessed=int(micros * 3.0e6), transcendentals=0),
            compiler_params=pltpu.CompilerParams(vmem_limit_bytes=GRANT),
        )(*scalars, *arrays)

    packed_shapes = [array(sh.rim_rows), array(sh.edge_rows)] + [array(sh.message_rows)] * (n - 1)

    def along_level(x, step):
        return permute(x, "level", lambda i: sh.sends_to(i, step))

    def exchange(messages, inside):
        got = [along_level(messages[i], i + 1) for i in range(n - 1)]
        got, inside = lax.optimization_barrier((got, inside))
        rim_got = sum(values[:sh.state_rim_rows] for values in got)
        return [rim_got, from_next(rim_got, "phase")] + got, inside

    other = from_next(flat, "phase")
    outs = call(
        functools.partial(pack_kernel, sh),
        [routes, tile_owner],
        [flat],
        ([array(sh.raw_rows)] if sh.deferred else []) + [array(sh.rows)] + packed_shapes,
        3,
        [table(n - 1, PICKS + 2 * sh.slots, I32)],
    )
    send_plan, outs = outs[0], outs[1:]
    if sh.deferred:
        raw_got, outs = from_partner(outs[0], "src", 0), outs[1:]
    start, rims, columns, messages = outs[0], outs[1], outs[2], outs[3:]
    plan, rates, paired, single, exits = call(
        functools.partial(prep_kernel, sh),
        [routes, tile_owner, tile_levels, service_rates, source_rates],
        [phase_rates, batch_rates],
        [
            table((BATCH // 2 + 1) * sh.phases, 6 * full, BF16),
            table(BATCH * sh.phases, 3 * full, BF16),
            array(sh.phases),
        ],
        2,
        [table(sh.slots, ROUTES + 15, I32), table(sh.states + 1, INFLOW + SOURCES)],
        [VM((2 * full, full), F32), VM((full, LANES), F32)],
    )

    def inner(first, values, other):
        shapes = [array(sh.rows)]
        if first and sh.deferred:
            shapes.append(array(sh.mid_rows))
        return call(functools.partial(inner_kernel, sh, first), [plan, rates], [paired, exits, values, other], shapes, 9)

    def halo(first, inside, values, rims, columns, got, extra):
        shapes = [array(sh.rows)]
        if first:
            shapes += ([array(sh.late_rows)] if sh.deferred else []) + packed_shapes
        return call(
            functools.partial(halo_kernel, sh, first),
            [plan, rates] + ([send_plan] if first else []),
            [single, inside, values, rims, from_next(rims, "phase"), columns] + got + extra,
            shapes,
            4,
        )

    if sh.deferred:
        inside, mid = inner(True, start, other)
        got_mid = from_partner(mid, "src", 0)
        got, inside = exchange(messages, inside)
        outs = halo(True, inside, start, rims, columns, got, [raw_got])
        once, late, rims, columns, messages = outs[0], outs[1], outs[2], outs[3], outs[4:]
        got_late = from_partner(late, "src", 0)
        (inside,) = inner(False, once, from_next(once, "phase"))
        got, inside = exchange(messages, inside)
        (twice,) = halo(False, inside, once, rims, columns, got, [raw_got, start])
        (result,) = call(
            functools.partial(join_kernel, sh), [plan, rates], [twice, got_mid, got_late], [array(sh.rows)], 3
        )
    else:
        (inside,) = inner(True, start, other)
        got, inside = exchange(messages, inside)
        extra = [from_partner(start, "src", bit) for bit in range(sh.cross)]
        outs = halo(True, inside, start, rims, columns, got, extra)
        once, rims, columns, messages = outs[0], outs[1], outs[2], outs[3:]
        (inside,) = inner(False, once, from_next(once, "phase"))
        got, inside = exchange(messages, inside)
        extra = [from_partner(once, "src", bit) for bit in range(sh.cross)]
        (result,) = halo(False, inside, once, rims, columns, got, extra)
    return result.reshape(block)


def solution(mesh):
    placed = (
        P(("groups", "level"), "src", "phase", None, None),
        P("groups", None),
        P("groups", None, None),
        P("groups"),
        P("groups", None),
        P("groups", None),
        P("groups", None),
        P("groups"),
    )
    return jax.shard_map(
        body,
        mesh=mesh,
        in_specs=placed,
        out_specs=P(("groups", "level"), "src", "phase", None, None),
        check_vma=False,
    )
```

```python
import functools

import jax
import jax.numpy as jnp
from jax import lax
from jax.experimental import pallas as pl
from jax.experimental.pallas import tpu as pltpu
from jax.sharding import PartitionSpec as P


BATCH = 16
SOURCES = 3
LANES = 128
F32 = jnp.float32
BF16 = jnp.bfloat16
I32 = jnp.int32
VM = pltpu.VMEM
SM = pltpu.SMEM
GRANT = 24 << 20

FEED, STAY, FEED_MORE, STAY_MORE, SQUARE, INFLOW = 0, 1, 2, 3, 4, 5
TILE, LEVEL_ONE, LEVEL_TWO, ROUTES = 0, 1, 2, 3
BELOW, ABOVE, LEFT, RIGHT, CORNER = 0, 1, 2, 3, 4
ROW, WANTED, LAST, PICKS = 0, 1, 2, 3


def permute(x, axis, pairs_of):
    return lax.ppermute(x, axis, [(i, pairs_of(i)) for i in range(lax.axis_size(axis))])


def from_next(x, axis):
    n = lax.axis_size(axis)
    return permute(x, axis, lambda i: (i - 1) % n)


def from_partner(x, axis, bit):
    return permute(x, axis, lambda i: i ^ 1 << bit)


class Shape:
    def __init__(self, block, tiles, levels):
        self.slots, self.states, self.phases, self.wide_two, self.wide_one = block
        self.tiles = tiles
        self.levels = levels
        self.units = self.slots * self.states
        self.rows = self.units * self.phases * self.wide_two
        self.rim_group = LANES // BATCH
        self.rim_parts = self.wide_two // self.rim_group
        self.state_rim_rows = self.states * self.rim_parts * self.phases
        self.rim_rows = self.slots * self.state_rim_rows
        self.edge_rows = self.units * self.phases
        self.lane_step = 2 * max(self.wide_two, BATCH)
        self.per_small = LANES // self.lane_step
        self.small_blocks = -(-self.states // self.per_small)
        self.small_rows_at = self.state_rim_rows + self.edge_rows
        self.message_rows = self.small_rows_at + self.small_blocks * self.phases
        self.bits = self.states.bit_length() - 1
        self.cross = SOURCES - self.bits
        self.deferred = self.cross == 1
        self.raw_end = self.states
        self.mid_end = self.units - self.states
        self.raw_rows = self.raw_end * self.wide_two * self.phases
        self.mid_rows = (self.mid_end - self.raw_end) * self.wide_two * self.phases
        self.ends_at = self.states * self.wide_two * self.phases
        self.rims_at = self.ends_at + self.mid_end * 2 * self.phases
        self.columns_at = self.rims_at + self.mid_end * self.rim_parts * self.phases
        self.per_column = LANES // self.wide_two
        self.late_rows = self.columns_at + -(-self.mid_end // self.per_column) * self.phases
        self.power = levels & (levels - 1) == 0

    def at(self, start):
        if not isinstance(start, int):
            start = pl.multiple_of(start, self.phases)
        return pl.ds(start, self.phases)

    def native(self, unit, u):
        return pl.ds(unit * self.phases * self.wide_two + u, self.phases, stride=self.wide_two)

    def by_level(self, unit, u):
        return self.at((unit * self.wide_two + u) * self.phases)

    def rim_at(self, unit, part):
        return self.at((unit * self.rim_parts + part) * self.phases)

    def small_at(self, state):
        return state // self.per_small, (state % self.per_small) * self.lane_step

    def sends_to(self, me, step):
        return me ^ step if self.power else (me + step) % self.levels

    def takes_from(self, me, step):
        return me ^ step if self.power else (me + self.levels - step) % self.levels


def lane_ids(shape):
    return lax.broadcasted_iota(I32, shape, len(shape) - 1)


def tile_at(owner, slot, tiles):
    found = jnp.int32(-1)
    for t in range(tiles):
        found = jnp.where(owner[t] == slot, t, found)
    return found


def route_of(routes, owner, tile, direction, slots):
    known = jnp.maximum(tile, 0)
    target = jnp.where(tile >= 0, routes[known, direction], -1)
    slot = owner[jnp.maximum(target, 0)]
    device = lax.div(slot, jnp.int32(slots))
    return target >= 0, device, slot - device * slots


def peer(sh, me, step, sending):
    if sh.power:
        return lax.bitwise_xor(me, jnp.int32(step))
    return lax.rem(me + (step if sending else sh.levels - step), jnp.int32(sh.levels))


def fill_send_plan(sh, routes, owner, plan):
    me = lax.axis_index("level")
    first = tile_at(owner, me * sh.slots, sh.tiles)
    count = jnp.int32(0)
    for k in range(sh.slots):
        count = count + jnp.where(tile_at(owner, me * sh.slots + k, sh.tiles) >= 0, 1, 0)
    for step in range(1, sh.levels):
        there = peer(sh, me, step, True)
        their_first = tile_at(owner, there * sh.slots, sh.tiles)
        lower = first < their_first
        found, device, _ = route_of(routes, owner, their_first, BELOW, sh.slots)
        plan[step - 1, ROW] = jnp.where(lower, sh.wide_two - 1, 0)
        plan[step - 1, WANTED] = jnp.where(jnp.logical_and(found, device == me), 1, 0)
        plan[step - 1, LAST] = (count - 1) * sh.states
        for k in range(sh.slots):
            tile = tile_at(owner, there * sh.slots + k, sh.tiles)
            _, _, left = route_of(routes, owner, tile, LEFT, sh.slots)
            _, _, right = route_of(routes, owner, tile, RIGHT, sh.slots)
            _, _, corner = route_of(routes, owner, tile, CORNER, sh.slots)
            plan[step - 1, PICKS + 2 * k] = jnp.where(lower, left, right) * sh.states
            plan[step - 1, PICKS + 2 * k + 1] = corner * sh.states


def add_packed(sh, lane, rims, column, u, values):
    part, q = u // sh.rim_group, u % sh.rim_group
    moved = pltpu.roll(values, (q * BATCH - (sh.wide_one - BATCH)) % LANES, 1)
    rims[part] = jnp.where(lax.div(lane, jnp.int32(BATCH)) == q, moved, rims[part])
    moved = pltpu.roll(values, u, 1) if u else values
    return jnp.where(lane == u, moved, column)


def write_messages(sh, plan, data, rims, columns, messages):
    phases, last_u = sh.phases, sh.wide_two - 1
    lane = lane_ids((phases, LANES))
    bottoms = [jnp.zeros((phases, LANES), F32) for _ in range(sh.small_blocks)]
    for s in range(sh.states):
        block, base = sh.small_at(s)
        values = columns[sh.at(s * phases), :]
        bottoms[block] = bottoms[block] + (pltpu.roll(values, base, 1) if base else values)
    for step in range(1, sh.levels):
        row = plan[step - 1, ROW]
        wanted = jnp.where(plan[step - 1, WANTED] > 0, 1.0, 0.0).astype(F32)
        last = plan[step - 1, LAST]
        for s in range(sh.states):
            for part in range(sh.rim_parts):
                messages[step - 1][sh.rim_at(s, part), :] = rims[sh.rim_at(last + s, part), :] * wanted
        small = list(bottoms)
        for k in range(sh.slots):
            slot, corner = plan[step - 1, PICKS + 2 * k], plan[step - 1, PICKS + 2 * k + 1]
            for s in range(sh.states):
                messages[step - 1][sh.at(sh.state_rim_rows + (k * sh.states + s) * phases), :] = data[sh.by_level(slot + s, row), :]
                block, base = sh.small_at(s)
                place = base + sh.lane_step // 2 + k
                moved = pltpu.roll(columns[sh.at((corner + s) * phases), :], (place - last_u) % LANES, 1)
                small[block] = jnp.where(lane == place, moved, small[block])
        for i, values in enumerate(small):
            messages[step - 1][sh.at(sh.small_rows_at + i * phases), :] = values


def pack_kernel(sh, routes, owner, data, send_plan, *outs):
    raw, (by_level, rims, columns, *messages) = (outs[0], outs[1:]) if sh.deferred else (None, outs)
    lane = lane_ids((sh.phases, LANES))
    fill_send_plan(sh, routes, owner, send_plan)

    def reorder(to_src, unit, carry):
        packed = [jnp.zeros((sh.phases, LANES), F32) for _ in range(sh.rim_parts)]
        column = jnp.zeros((sh.phases, LANES), F32)
        for u in range(sh.wide_two):
            values = data[sh.native(unit, u), :]
            by_level[sh.by_level(unit, u), :] = values
            if to_src:
                raw[sh.by_level(unit, u), :] = values
            column = add_packed(sh, lane, packed, column, u, values)
        for part, values in enumerate(packed):
            rims[sh.rim_at(unit, part), :] = values
        columns[sh.at(unit * sh.phases), :] = column
        return carry

    first = sh.raw_end if sh.deferred else 0
    if sh.deferred:
        lax.fori_loop(0, first, functools.partial(reorder, True), 0)
    lax.fori_loop(first, sh.units, functools.partial(reorder, False), 0)
    write_messages(sh, send_plan, by_level, rims, columns, messages)


def source_scalars(sources, scale, state):
    feed = jnp.float32(0.0)
    outflow = jnp.float32(0.0)
    inflow = []
    for k in range(SOURCES):
        on = lax.rem(lax.shift_right_logical(state, jnp.int32(k)), jnp.int32(2)) == 1
        turn_on, turn_off, arrive = sources[k, 0], sources[k, 1], sources[k, 2]
        feed = feed + jnp.where(on, arrive, 0.0)
        outflow = outflow + jnp.where(on, turn_off, turn_on)
        inflow.append(jnp.where(on, turn_on, turn_off) * scale)
    return feed * scale, outflow * scale, inflow


def prep_kernel(sh, routes, owner, levels_t, service, sources, phase_rates, batch_rates, plan, rates, paired, rim_paired,
                exits, turned, wide):
    me = lax.axis_index("level")
    for k in range(sh.slots):
        tile = tile_at(owner, me * sh.slots + k, sh.tiles)
        known = jnp.maximum(tile, 0)
        plan[k, TILE] = tile
        plan[k, LEVEL_ONE] = levels_t[known, 0]
        plan[k, LEVEL_TWO] = levels_t[known, 1]
        for r in range(5):
            found, device, slot = route_of(routes, owner, tile, r, sh.slots)
            kind = jnp.int32(1)
            for step in range(1, sh.levels):
                kind = jnp.where(device == peer(sh, me, step, False), step + 1, kind)
            plan[k, ROUTES + 3 * r] = jnp.where(found, kind, 0)
            plan[k, ROUTES + 3 * r + 1] = slot * sh.states
            plan[k, ROUTES + 3 * r + 2] = jnp.where(slot == 0, 1, 0)

    phases, full = sh.phases, phase_rates.shape[0]
    start = lax.axis_index("phase") * phases
    rows_here = pl.ds(pl.multiple_of(start, phases), phases)
    shape = (full, full)
    moving = phase_rates[...]
    moving = jnp.where(lax.broadcasted_iota(I32, shape, 0) == lax.broadcasted_iota(I32, shape, 1), 0.0, moving)
    total = moving
    for b in range(BATCH):
        total = total + batch_rates[b]
    leaving = jnp.sum(total, axis=1, keepdims=True)
    sources_top = jnp.float32(0.0)
    for k in range(SOURCES):
        sources_top = sources_top + jnp.maximum(sources[k, 2] + sources[k, 1], sources[k, 0])
    uniform = jnp.max(leaving) + (service[0] + service[1] + sources_top)
    inverse = 1.0 / jnp.full((phases, LANES), uniform, F32)
    scale = jnp.max(inverse)
    wide[...] = jnp.broadcast_to(leaving, (full, LANES))
    exits[...] = wide[rows_here, :] * inverse

    base = lax.axis_index("src") * sh.states
    rates[sh.states, 0] = service[0] * scale
    rates[sh.states, 1] = service[1] * scale
    for s in range(sh.states):
        state = base + s
        feed, outflow, inflow = source_scalars(sources, scale, state)
        rates[s, FEED] = feed
        rates[s, STAY] = 1.0 - feed - outflow
        for k in range(SOURCES):
            rates[s, INFLOW + k] = inflow[k]
        if sh.deferred:
            there = lax.bitwise_xor(state, jnp.int32(1 << sh.bits))
            feed_there, outflow_there, inflow_there = source_scalars(sources, scale, there)
            rates[s, FEED_MORE] = feed_there - feed
            rates[s, STAY_MORE] = (feed + outflow) - (feed_there + outflow_there)
            rates[s, SQUARE] = inflow[sh.bits] * inflow_there[sh.bits]

    for b in range(BATCH + 2):
        if b <= BATCH:
            values = (moving if b == 0 else batch_rates[b - 1]) * scale
            turned[0:full, :] = values
            turned[full:2 * full, :] = values
            turned[0:full, :] = turned[pl.ds(pl.multiple_of(start, phases), full), :].T
            values = turned[rows_here, :]
            high = values.astype(BF16)
            low = (values - high.astype(F32)).astype(BF16)
        else:
            high = jnp.zeros((phases, full), BF16)
            low = high
        parts = (high, low, high)
        for i, part in enumerate(parts):
            if 1 <= b <= BATCH:
                column = ((b - 1) % 2) * 3 * full + i * full
                rim_paired[((b - 1) // 2) * phases:((b - 1) // 2 + 1) * phases, column:column + full] = part
            column = (b % 2) * 3 * full + i * full
            paired[(b // 2) * phases:(b // 2 + 1) * phases, column:column + full] = part


def split(values):
    high = values.astype(BF16)
    low = (values - high.astype(F32)).astype(BF16)
    return [high, high, low]


def inner_kernel(sh, first, plan, rates, weights, exits, own, other, *outs):
    phases = sh.phases
    out = outs[0]
    sent = outs[1] if first and sh.deferred else None
    other_at = sh.native if first else sh.by_level
    serve_one, serve_two = rates[sh.states, 0], rates[sh.states, 1]
    lane = lane_ids((phases, LANES))
    inner_one = jnp.where(lane == LANES - 1, 0.0, serve_one)
    later = lane_ids((weights.shape[1] // 6, LANES)) > 0

    def unit_step(sending, unit, carry):
        k = lax.div(unit, jnp.int32(sh.states))
        s = unit - k * sh.states
        a, c = plan[k, LEVEL_ONE], plan[k, LEVEL_TWO]
        feed = rates[s, FEED]
        stay = rates[s, STAY] - exits[...] - jnp.where(jnp.logical_or(lane > 0, a > 0), serve_one, 0.0)
        for pair in range(sh.wide_two // 2):
            columns = []
            for u in (2 * pair, 2 * pair + 1):
                values = jnp.concatenate([own[sh.by_level(unit, u), :], other[other_at(unit, u), :]], axis=0)
                columns.append(jnp.concatenate(split(values) + split(jnp.where(later, pltpu.roll(values, 1, 1), 0.0)), axis=0))
            product = jnp.dot(weights[...], jnp.concatenate(columns, axis=1), preferred_element_type=F32)
            for j, u in enumerate((2 * pair, 2 * pair + 1)):
                lanes = slice(j * LANES, (j + 1) * LANES)
                total = product[0:phases, lanes]
                for b in range(1, BATCH // 2 + 1):
                    moved = pltpu.roll(product[b * phases:(b + 1) * phases, lanes], 2 * b, 1)
                    total = total + jnp.where(lane >= 2 * b, moved, 0.0)
                here = own[sh.by_level(unit, u), :]
                two = serve_two if u else jnp.where(c > 0, serve_two, 0.0)
                total = total + (stay - two) * here
                if u:
                    prev = own[sh.by_level(unit, u - 1), :]
                    total = total + inner_one * pltpu.roll(prev, LANES - 1, 1) + feed * prev
                if u + 1 < sh.wide_two:
                    total = total + serve_two * own[sh.by_level(unit, u + 1), :]
                for bit in range(sh.bits):
                    flipped = unit - s + lax.bitwise_xor(s, jnp.int32(1 << bit))
                    total = total + rates[s, INFLOW + bit] * own[sh.by_level(flipped, u), :]
                out[sh.by_level(unit, u), :] = total
                if sending:
                    more = rates[s, STAY_MORE] * here
                    if u:
                        more = more + rates[s, FEED_MORE] * prev
                    sent[sh.by_level(unit - sh.raw_end, u), :] = 2.0 * total + more
        return carry

    if sent is not None:
        lax.fori_loop(sh.raw_end, sh.mid_end, functools.partial(unit_step, True), 0)
        lax.fori_loop(0, sh.raw_end, functools.partial(unit_step, False), 0)
        lax.fori_loop(sh.mid_end, sh.units, functools.partial(unit_step, False), 0)
    else:
        lax.fori_loop(0, sh.units, functools.partial(unit_step, False), 0)


def halo_kernel(sh, first, *refs):
    refs = list(refs)
    n, phases, last_u = sh.levels, sh.phases, sh.wide_two - 1
    plan, rates = refs[:2]
    refs = refs[2:]
    send_plan = refs.pop(0) if first else None
    weights, inner, own, rims_own, rims_other, columns_own, rim_got, rim_other = refs[:8]
    refs = refs[8:]
    edges, refs = refs[:n - 1], refs[n - 1:]
    raw = 0 if sh.deferred else sh.cross
    partners, refs = refs[:raw], refs[raw:]
    raw_got = refs.pop(0) if sh.deferred else None
    start_values = refs.pop(0) if sh.deferred and not first else None
    out = refs.pop(0)
    sent = refs.pop(0) if sh.deferred and first else None
    rims_out, columns_out = (refs.pop(0), refs.pop(0)) if first else (None, None)
    serve_one, serve_two = rates[sh.states, 0], rates[sh.states, 1]
    lane = lane_ids((phases, LANES))
    group_lane = lax.rem(lane, jnp.int32(BATCH))
    zero = jnp.zeros((phases, LANES), F32)
    if sent is not None:
        for start in range(sh.columns_at, sh.late_rows, phases):
            sent[start:start + phases, :] = zero

    def rim_product(halves):
        columns = []
        for pair in halves:
            values = jnp.concatenate(pair, axis=0)
            ends = lax.rem(lane_ids(values.shape), jnp.int32(BATCH)) == BATCH - 1
            moved = jnp.where(ends, 0.0, pltpu.roll(values, LANES - 1, 1))
            columns.append(jnp.concatenate(split(moved) + split(values), axis=0))
        product = jnp.dot(weights[...], jnp.concatenate(columns, axis=1), preferred_element_type=F32)
        sums = []
        for i in range(len(halves)):
            total = product[(BATCH // 2 - 1) * phases:(BATCH // 2) * phases, i * LANES:(i + 1) * LANES]
            for j in range(BATCH // 2 - 1):
                block = product[j * phases:(j + 1) * phases, i * LANES:(i + 1) * LANES]
                moved = pltpu.roll(block, (2 * j + 2 - BATCH) % LANES, 1)
                total = total + jnp.where(group_lane <= 2 * j + 1, moved, 0.0)
            sums.append(total)
        return sums

    def unit_step(group, unit, carry):
        k = lax.div(unit, jnp.int32(sh.states))
        s = unit - k * sh.states

        def kind(which):
            return plan[k, ROUTES + 3 * which]

        def beside(which):
            return plan[k, ROUTES + 3 * which + 1] + s

        def kept(which):
            return jnp.where(plan[k, ROUTES + 3 * which + 2] > 0, 0.0, 1.0).astype(F32)

        def number(flag):
            return jnp.where(flag, 1.0, 0.0).astype(F32)

        def remote(which, rows):
            value = zero
            for step in range(1, n):
                value = jnp.where(kind(which) == step + 1, edges[step - 1][rows, :], value)
            return value

        small_base = lax.rem(s, jnp.int32(sh.per_small)) * sh.lane_step
        small_at = sh.at(sh.small_rows_at + lax.div(s, jnp.int32(sh.per_small)) * phases)
        edge_at = sh.at(sh.state_rim_rows + unit * phases)
        left = jnp.where(kind(LEFT) == 1, own[sh.by_level(beside(LEFT), last_u), :], remote(LEFT, edge_at))
        right = jnp.where(kind(RIGHT) == 1, own[sh.by_level(beside(RIGHT), 0), :], remote(RIGHT, edge_at))
        above = jnp.where(
            kind(ABOVE) == 1,
            columns_own[sh.at(beside(ABOVE) * phases), :],
            pltpu.roll(remote(ABOVE, small_at), LANES - small_base, 1),
        )
        above = jnp.where(lane < sh.wide_two, above, 0.0) * serve_one
        corner = jnp.where(
            kind(CORNER) == 1,
            pltpu.roll(columns_own[sh.at(beside(CORNER) * phases), :], LANES - 1 - last_u, 1),
            pltpu.roll(remote(CORNER, small_at), LANES - 1 - (small_base + sh.lane_step // 2 + k), 1),
        )
        corner = jnp.where(lane == LANES - 1, corner, 0.0) * serve_one
        shifted = jnp.where(lane == LANES - 1, 0.0, pltpu.roll(left, LANES - 1, 1)) * serve_one
        below_local, below_remote = number(kind(BELOW) == 1), number(kind(BELOW) > 1)
        under = []
        for part in range(sh.rim_parts):
            under.append([
                rims_own[sh.rim_at(beside(BELOW), part), :] * below_local + rim_got[sh.rim_at(s, part), :] * below_remote,
                rims_other[sh.rim_at(beside(BELOW), part), :] * below_local
                + rim_other[sh.rim_at(s, part), :] * below_remote,
            ])
        feed = rates[s, FEED]
        rims = rim_product(under)
        if group is not None:
            keep_left = kept(LEFT)
            rim_scale, column_scale = 2.0 * kept(BELOW), 2.0 * kept(ABOVE)
            sent_first = (2.0 * keep_left) * (shifted + feed * left) + (2.0 * kept(CORNER)) * corner
            sent_first = sent_first + ((2.0 * keep_left - 1.0) * rates[s, FEED_MORE]) * left
            sent_last = (2.0 * kept(RIGHT) * serve_two) * right
            if group != "last":
                sent[sh.at(sh.ends_at + 2 * unit * phases), :] = sent_first
                sent[sh.at(sh.ends_at + (2 * unit + 1) * phases), :] = sent_last
                for part in range(sh.rim_parts):
                    sent[sh.at(sh.rims_at + (unit * sh.rim_parts + part) * phases), :] = rim_scale * rims[part]
                place = sh.at(sh.columns_at + lax.div(unit, jnp.int32(sh.per_column)) * phases)
                base = lax.rem(unit, jnp.int32(sh.per_column)) * sh.wide_two
                sent[place, :] = sent[place, :] + column_scale * pltpu.roll(above, base, 1)
        packed, packed_column = [zero] * sh.rim_parts, zero
        for u in range(sh.wide_two):
            part, q = u // sh.rim_group, u % sh.rim_group

            inside = inner[sh.by_level(unit, u), :]
            rim = jnp.where(lane < BATCH, pltpu.roll(rims[part], LANES - q * BATCH, 1) if q else rims[part], 0.0)
            edge = jnp.where(lane == LANES - 1, pltpu.roll(above, LANES - u, 1), 0.0) if u else zero
            total = inside + rim + edge
            if u == 0:
                total = total + shifted + corner + feed * left
            if u == last_u:
                total = total + serve_two * right
            for bit, values in enumerate(partners):
                total = total + rates[s, INFLOW + sh.bits + bit] * values[sh.by_level(unit, u), :]
            if group == "raw":
                total = total + (2.0 * rates[s, INFLOW + sh.bits]) * raw_got[sh.by_level(unit, u), :]
            if start_values is not None:
                total = total + rates[s, SQUARE] * start_values[sh.by_level(unit, u), :]
            if raw_got is not None and carry == "raw":
                more = rates[s, STAY_MORE] * raw_got[sh.by_level(unit, u), :]
                if u:
                    more = more + rates[s, FEED_MORE] * raw_got[sh.by_level(unit, u - 1), :]
                total = total + rates[s, INFLOW + sh.bits] * more
            if first:
                packed_column = add_packed(sh, lane, packed, packed_column, u, total)
            if first or sh.deferred:
                out[sh.by_level(unit, u), :] = total
            else:
                out[sh.native(unit, u), :] = jnp.where(plan[k, TILE] >= 0, total, 0.0)
            if group == "last":
                value = 2.0 * inside + rim_scale * rim + column_scale * edge
                value = value + rates[s, STAY_MORE] * own[sh.by_level(unit, u), :]
                if u:
                    value = value + rates[s, FEED_MORE] * own[sh.by_level(unit, u - 1), :]
                else:
                    value = value + sent_first
                if u == last_u:
                    value = value + sent_last
                sent[sh.by_level(unit - sh.mid_end, u), :] = value
        if first:
            for part in range(sh.rim_parts):
                rims_out[sh.rim_at(unit, part), :] = packed[part]
            columns_out[sh.at(unit * phases), :] = packed_column

    def sweep(start, stop, group, mark=None):
        wished = 2 if first else 4
        many = wished if (stop - start) % wished == 0 else 1

        def step(index, carry):
            for j in range(many):
                unit_step(group, start + index * many + j, mark)
            return carry

        lax.fori_loop(0, (stop - start) // many, step, 0)

    if sent is not None:
        sweep(0, sh.raw_end, "raw")
        sweep(sh.raw_end, sh.mid_end, "mid")
        sweep(sh.mid_end, sh.units, "last")
    elif sh.deferred:
        sweep(0, sh.raw_end, None, "raw")
        sweep(sh.raw_end, sh.units, None)
    else:
        sweep(0, sh.units, None)
    if first:
        write_messages(sh, send_plan, out, rims_out, columns_out, refs)


def join_kernel(sh, plan, rates, stepped, got_mid, got_late, out):
    phases, last_u = sh.phases, sh.wide_two - 1
    lane = lane_ids((phases, LANES))
    inflow = rates[0, INFLOW + sh.bits]

    def unit_step(group, unit, carry):
        filled = plan[lax.div(unit, jnp.int32(sh.states)), TILE] >= 0
        if group != "last":
            rims = [
                got_late[sh.at(sh.rims_at + (unit * sh.rim_parts + part) * phases), :] for part in range(sh.rim_parts)
            ]
            column = got_late[sh.at(sh.columns_at + lax.div(unit, jnp.int32(sh.per_column)) * phases), :]
            base = lax.rem(unit, jnp.int32(sh.per_column)) * sh.wide_two
        for u in range(sh.wide_two):
            if group == "last":
                got = got_late[sh.by_level(unit - sh.mid_end, u), :]
            else:
                part, q = u // sh.rim_group, u % sh.rim_group
                got = jnp.where(lane < BATCH, pltpu.roll(rims[part], LANES - q * BATCH, 1) if q else rims[part], 0.0)
                if u:
                    got = jnp.where(lane == LANES - 1, pltpu.roll(column, LANES - (base + u), 1), got)
                if u in (0, last_u):
                    got = got + got_late[sh.at(sh.ends_at + (2 * unit + (1 if u else 0)) * phases), :]
                if group == "mid":
                    got = got + got_mid[sh.by_level(unit - sh.raw_end, u), :]
            total = stepped[sh.by_level(unit, u), :] + inflow * got
            out[sh.native(unit, u), :] = jnp.where(filled, total, 0.0)
        return carry

    lax.fori_loop(0, sh.raw_end, functools.partial(unit_step, "raw"), 0)
    lax.fori_loop(sh.raw_end, sh.mid_end, functools.partial(unit_step, "mid"), 0)
    lax.fori_loop(sh.mid_end, sh.units, functools.partial(unit_step, "last"), 0)


def body(
    state_values,
    phase_rates,
    batch_rates,
    service_rates,
    source_rates,
    tile_levels,
    routes,
    tile_owner,
):
    block = state_values.shape
    sh = Shape(block, tile_owner.shape[0], lax.axis_size("level"))
    n, full = sh.levels, phase_rates.shape[0]
    flat = state_values.reshape(sh.rows, LANES)
    smem, vmem = pl.BlockSpec(memory_space=SM), pl.BlockSpec(memory_space=VM)

    def array(rows):
        return jax.ShapeDtypeStruct((rows, LANES), F32)

    def table(rows, columns, dtype=F32):
        return jax.ShapeDtypeStruct((rows, columns), dtype)

    def call(kernel, scalars, arrays, shapes, micros, scalar_shapes=(), scratch=()):
        return pl.pallas_call(
            kernel,
            out_shape=tuple(scalar_shapes) + tuple(shapes),
            in_specs=[smem] * len(scalars) + [vmem] * len(arrays),
            out_specs=tuple([smem] * len(scalar_shapes) + [vmem] * len(shapes)),
            scratch_shapes=list(scratch),
            cost_estimate=pl.CostEstimate(flops=0, bytes_accessed=int(micros * 3.0e6), transcendentals=0),
            compiler_params=pltpu.CompilerParams(vmem_limit_bytes=GRANT),
        )(*scalars, *arrays)

    packed_shapes = [array(sh.rim_rows), array(sh.edge_rows)] + [array(sh.message_rows)] * (n - 1)

    def along_level(x, step):
        return permute(x, "level", lambda i: sh.sends_to(i, step))

    def exchange(messages, inside):
        got = [along_level(messages[i], i + 1) for i in range(n - 1)]
        got, inside = lax.optimization_barrier((got, inside))
        rim_got = sum(values[:sh.state_rim_rows] for values in got)
        return [rim_got, from_next(rim_got, "phase")] + got, inside

    other = from_next(flat, "phase")
    outs = call(
        functools.partial(pack_kernel, sh),
        [routes, tile_owner],
        [flat],
        ([array(sh.raw_rows)] if sh.deferred else []) + [array(sh.rows)] + packed_shapes,
        3,
        [table(n - 1, PICKS + 2 * sh.slots, I32)],
    )
    send_plan, outs = outs[0], outs[1:]
    if sh.deferred:
        raw_got, outs = from_partner(outs[0], "src", 0), outs[1:]
    start, rims, columns, messages = outs[0], outs[1], outs[2], outs[3:]
    plan, rates, paired, rim_paired, exits = call(
        functools.partial(prep_kernel, sh),
        [routes, tile_owner, tile_levels, service_rates, source_rates],
        [phase_rates, batch_rates],
        [
            table((BATCH // 2 + 1) * sh.phases, 6 * full, BF16),
            table((BATCH // 2) * sh.phases, 6 * full, BF16),
            array(sh.phases),
        ],
        2,
        [table(sh.slots, ROUTES + 15, I32), table(sh.states + 1, INFLOW + SOURCES)],
        [VM((2 * full, full), F32), VM((full, LANES), F32)],
    )

    def inner(first, values, other):
        shapes = [array(sh.rows)]
        if first and sh.deferred:
            shapes.append(array(sh.mid_rows))
        return call(functools.partial(inner_kernel, sh, first), [plan, rates], [paired, exits, values, other], shapes, 9)

    def halo(first, inside, values, rims, columns, got, extra):
        shapes = [array(sh.rows)]
        if first:
            shapes += ([array(sh.late_rows)] if sh.deferred else []) + packed_shapes
        rims_other = from_next(rims, "phase")
        return call(
            functools.partial(halo_kernel, sh, first),
            [plan, rates] + ([send_plan] if first else []),
            [rim_paired, inside, values, rims, rims_other, columns] + got + extra,
            shapes,
            4,
        )

    if sh.deferred:
        inside, mid = inner(True, start, other)
        got_mid = from_partner(mid, "src", 0)
        got, inside = exchange(messages, inside)
        outs = halo(True, inside, start, rims, columns, got, [raw_got])
        once, late, rims, columns, messages = outs[0], outs[1], outs[2], outs[3], outs[4:]
        got_late = from_partner(late, "src", 0)
        other = from_next(once, "phase")
        (inside,) = inner(False, once, other)
        got, inside = exchange(messages, inside)
        (twice,) = halo(False, inside, once, rims, columns, got, [raw_got, start])
        (result,) = call(
            functools.partial(join_kernel, sh), [plan, rates], [twice, got_mid, got_late], [array(sh.rows)], 3
        )
    else:
        (inside,) = inner(True, start, other)
        got, inside = exchange(messages, inside)
        extra = [from_partner(start, "src", bit) for bit in range(sh.cross)]
        outs = halo(True, inside, start, rims, columns, got, extra)
        once, rims, columns, messages = outs[0], outs[1], outs[2], outs[3:]
        (inside,) = inner(False, once, from_next(once, "phase"))
        got, inside = exchange(messages, inside)
        extra = [from_partner(once, "src", bit) for bit in range(sh.cross)]
        (result,) = halo(False, inside, once, rims, columns, got, extra)
    return result.reshape(block)


def solution(mesh):
    placed = (
        P(("groups", "level"), "src", "phase", None, None),
        P("groups", None),
        P("groups", None, None),
        P("groups"),
        P("groups", None),
        P("groups", None),
        P("groups", None),
        P("groups"),
    )

    return jax.shard_map(
        body,
        mesh=mesh,
        in_specs=placed,
        out_specs=P(("groups", "level"), "src", "phase", None, None),
        check_vma=False,
    )
```

```python
import functools

import jax
import jax.numpy as jnp
from jax import lax
from jax.experimental import pallas as pl
from jax.experimental.pallas import tpu as pltpu
from jax.sharding import PartitionSpec as P


BATCH = 16
SOURCES = 3
LANES = 128
F32 = jnp.float32
BF16 = jnp.bfloat16
I32 = jnp.int32
VM = pltpu.VMEM
SM = pltpu.SMEM
GRANT = 24 << 20
PACK_TURN, JOIN_TURN = 4, 4

FEED, STAY, FEED_MORE, STAY_MORE, SQUARE, INFLOW = 0, 1, 2, 3, 4, 5
TILE, LEVEL_ONE, LEVEL_TWO, ROUTES = 0, 1, 2, 3
BELOW, ABOVE, LEFT, RIGHT, CORNER = 0, 1, 2, 3, 4
ROW, WANTED, LAST, PICKS = 0, 1, 2, 3


def permute(x, axis, pairs_of):
    return lax.ppermute(x, axis, [(i, pairs_of(i)) for i in range(lax.axis_size(axis))])


def from_next(x, axis):
    n = lax.axis_size(axis)
    return permute(x, axis, lambda i: (i - 1) % n)


def from_partner(x, axis, bit):
    return permute(x, axis, lambda i: i ^ 1 << bit)


class Shape:
    def __init__(self, block, tiles, levels):
        self.slots, self.states, self.phases, self.wide_two, self.wide_one = block
        self.tiles = tiles
        self.levels = levels
        self.units = self.slots * self.states
        self.rows = self.units * self.phases * self.wide_two
        self.rim_group = LANES // BATCH
        self.rim_parts = self.wide_two // self.rim_group
        self.state_rim_rows = self.states * self.rim_parts * self.phases
        self.rim_rows = self.slots * self.state_rim_rows
        self.edge_rows = self.units * self.phases
        self.lane_step = 2 * max(self.wide_two, BATCH)
        self.per_small = LANES // self.lane_step
        self.small_blocks = -(-self.states // self.per_small)
        self.small_rows_at = self.state_rim_rows + self.edge_rows
        self.message_rows = self.small_rows_at + self.small_blocks * self.phases
        self.bits = self.states.bit_length() - 1
        self.cross = SOURCES - self.bits
        self.deferred = self.cross == 1
        self.raw_end = self.states
        self.mid_end = self.units - self.states
        self.raw_rows = self.raw_end * self.wide_two * self.phases
        self.mid_rows = (self.mid_end - self.raw_end) * self.wide_two * self.phases
        self.ends_at = self.states * self.wide_two * self.phases
        self.rims_at = self.ends_at + self.mid_end * 2 * self.phases
        self.columns_at = self.rims_at + self.mid_end * self.rim_parts * self.phases
        self.per_column = LANES // self.wide_two
        self.late_rows = self.columns_at + -(-self.mid_end // self.per_column) * self.phases
        self.power = levels & (levels - 1) == 0

    def at(self, start):
        if not isinstance(start, int):
            start = pl.multiple_of(start, self.phases)
        return pl.ds(start, self.phases)

    def native(self, unit, u):
        return pl.ds(unit * self.phases * self.wide_two + u, self.phases, stride=self.wide_two)

    def by_level(self, unit, u):
        return self.at((unit * self.wide_two + u) * self.phases)

    def rim_at(self, unit, part):
        return self.at((unit * self.rim_parts + part) * self.phases)

    def small_at(self, state):
        return state // self.per_small, (state % self.per_small) * self.lane_step

    def sends_to(self, me, step):
        return me ^ step if self.power else (me + step) % self.levels

    def takes_from(self, me, step):
        return me ^ step if self.power else (me + self.levels - step) % self.levels


def sweep(start, stop, wished, visit):
    many = wished if (stop - start) % wished == 0 else 1

    def turn(index, carry):
        for j in range(many):
            visit(start + index * many + j)
        return carry

    lax.fori_loop(0, (stop - start) // many, turn, 0)


def lane_ids(shape):
    return lax.broadcasted_iota(I32, shape, len(shape) - 1)


def tile_at(owner, slot, tiles):
    found = jnp.int32(-1)
    for t in range(tiles):
        found = jnp.where(owner[t] == slot, t, found)
    return found


def route_of(routes, owner, tile, direction, slots):
    known = jnp.maximum(tile, 0)
    target = jnp.where(tile >= 0, routes[known, direction], -1)
    slot = owner[jnp.maximum(target, 0)]
    device = lax.div(slot, jnp.int32(slots))
    return target >= 0, device, slot - device * slots


def peer(sh, me, step, sending):
    if sh.power:
        return lax.bitwise_xor(me, jnp.int32(step))
    return lax.rem(me + (step if sending else sh.levels - step), jnp.int32(sh.levels))


def fill_send_plan(sh, routes, owner, plan):
    me = lax.axis_index("level")
    first = tile_at(owner, me * sh.slots, sh.tiles)
    count = jnp.int32(0)
    for k in range(sh.slots):
        count = count + jnp.where(tile_at(owner, me * sh.slots + k, sh.tiles) >= 0, 1, 0)
    for step in range(1, sh.levels):
        there = peer(sh, me, step, True)
        their_first = tile_at(owner, there * sh.slots, sh.tiles)
        lower = first < their_first
        found, device, _ = route_of(routes, owner, their_first, BELOW, sh.slots)
        plan[step - 1, ROW] = jnp.where(lower, sh.wide_two - 1, 0)
        plan[step - 1, WANTED] = jnp.where(jnp.logical_and(found, device == me), 1, 0)
        plan[step - 1, LAST] = (count - 1) * sh.states
        for k in range(sh.slots):
            tile = tile_at(owner, there * sh.slots + k, sh.tiles)
            _, _, left = route_of(routes, owner, tile, LEFT, sh.slots)
            _, _, right = route_of(routes, owner, tile, RIGHT, sh.slots)
            _, _, corner = route_of(routes, owner, tile, CORNER, sh.slots)
            plan[step - 1, PICKS + 2 * k] = jnp.where(lower, left, right) * sh.states
            plan[step - 1, PICKS + 2 * k + 1] = corner * sh.states


def add_packed(sh, lane, rims, column, u, values):
    part, q = u // sh.rim_group, u % sh.rim_group
    moved = pltpu.roll(values, (q * BATCH - (sh.wide_one - BATCH)) % LANES, 1)
    rims[part] = jnp.where(lax.div(lane, jnp.int32(BATCH)) == q, moved, rims[part])
    moved = pltpu.roll(values, u, 1) if u else values
    return jnp.where(lane == u, moved, column)


def write_messages(sh, plan, data, rims, columns, messages):
    phases, last_u = sh.phases, sh.wide_two - 1
    lane = lane_ids((phases, LANES))
    bottoms = [jnp.zeros((phases, LANES), F32) for _ in range(sh.small_blocks)]
    for s in range(sh.states):
        block, base = sh.small_at(s)
        values = columns[sh.at(s * phases), :]
        bottoms[block] = bottoms[block] + (pltpu.roll(values, base, 1) if base else values)
    for step in range(1, sh.levels):
        row = plan[step - 1, ROW]
        wanted = jnp.where(plan[step - 1, WANTED] > 0, 1.0, 0.0).astype(F32)
        last = plan[step - 1, LAST]
        for s in range(sh.states):
            for part in range(sh.rim_parts):
                messages[step - 1][sh.rim_at(s, part), :] = rims[sh.rim_at(last + s, part), :] * wanted
        small = list(bottoms)
        for k in range(sh.slots):
            slot, corner = plan[step - 1, PICKS + 2 * k], plan[step - 1, PICKS + 2 * k + 1]
            for s in range(sh.states):
                messages[step - 1][sh.at(sh.state_rim_rows + (k * sh.states + s) * phases), :] = data[sh.by_level(slot + s, row), :]
                block, base = sh.small_at(s)
                place = base + sh.lane_step // 2 + k
                moved = pltpu.roll(columns[sh.at((corner + s) * phases), :], (place - last_u) % LANES, 1)
                small[block] = jnp.where(lane == place, moved, small[block])
        for i, values in enumerate(small):
            messages[step - 1][sh.at(sh.small_rows_at + i * phases), :] = values


def pack_kernel(sh, routes, owner, data_hbm, send_plan, *outs):
    outs, (data, arrived) = outs[:-2], outs[-2:]
    raw, (by_level, rims, columns, *messages) = (outs[0], outs[1:]) if sh.deferred else (None, outs)
    lane = lane_ids((sh.phases, LANES))
    size = sh.rows // sh.slots
    copies = [
        pltpu.make_async_copy(data_hbm.at[pl.ds(k * size, size)], data.at[pl.ds(k * size, size)], arrived.at[k])
        for k in range(sh.slots)
    ]
    for copy in copies:
        copy.start()
    fill_send_plan(sh, routes, owner, send_plan)

    def reorder(to_src, unit):
        packed = [jnp.zeros((sh.phases, LANES), F32) for _ in range(sh.rim_parts)]
        column = jnp.zeros((sh.phases, LANES), F32)
        for u in range(sh.wide_two):
            values = data[sh.native(unit, u), :]
            by_level[sh.by_level(unit, u), :] = values
            if to_src:
                raw[sh.by_level(unit, u), :] = values
            column = add_packed(sh, lane, packed, column, u, values)
        for part, values in enumerate(packed):
            rims[sh.rim_at(unit, part), :] = values
        columns[sh.at(unit * sh.phases), :] = column

    for k, copy in enumerate(copies):
        copy.wait()
        sweep(k * sh.states, (k + 1) * sh.states, PACK_TURN, functools.partial(reorder, sh.deferred and k == 0))
    write_messages(sh, send_plan, by_level, rims, columns, messages)


def source_scalars(sources, scale, state):
    feed = jnp.float32(0.0)
    outflow = jnp.float32(0.0)
    inflow = []
    for k in range(SOURCES):
        on = lax.rem(lax.shift_right_logical(state, jnp.int32(k)), jnp.int32(2)) == 1
        turn_on, turn_off, arrive = sources[k, 0], sources[k, 1], sources[k, 2]
        feed = feed + jnp.where(on, arrive, 0.0)
        outflow = outflow + jnp.where(on, turn_off, turn_on)
        inflow.append(jnp.where(on, turn_on, turn_off) * scale)
    return feed * scale, outflow * scale, inflow


def prep_kernel(sh, routes, owner, levels_t, service, sources, phase_rates, batch_rates, plan, rates, paired, rim_paired,
                exits, turned, wide):
    me = lax.axis_index("level")
    for k in range(sh.slots):
        tile = tile_at(owner, me * sh.slots + k, sh.tiles)
        known = jnp.maximum(tile, 0)
        plan[k, TILE] = tile
        plan[k, LEVEL_ONE] = levels_t[0, known]
        plan[k, LEVEL_TWO] = levels_t[1, known]
        for r in range(5):
            found, device, slot = route_of(routes, owner, tile, r, sh.slots)
            kind = jnp.int32(1)
            for step in range(1, sh.levels):
                kind = jnp.where(device == peer(sh, me, step, False), step + 1, kind)
            plan[k, ROUTES + 3 * r] = jnp.where(found, kind, 0)
            plan[k, ROUTES + 3 * r + 1] = slot * sh.states
            plan[k, ROUTES + 3 * r + 2] = jnp.where(slot == 0, 1, 0)

    phases, full = sh.phases, phase_rates.shape[0]
    start = lax.axis_index("phase") * phases
    rows_here = pl.ds(pl.multiple_of(start, phases), phases)
    shape = (full, full)
    moving = phase_rates[...]
    moving = jnp.where(lax.broadcasted_iota(I32, shape, 0) == lax.broadcasted_iota(I32, shape, 1), 0.0, moving)
    total = moving
    for b in range(BATCH):
        total = total + batch_rates[b]
    leaving = jnp.sum(total, axis=1, keepdims=True)
    sources_top = jnp.float32(0.0)
    for k in range(SOURCES):
        sources_top = sources_top + jnp.maximum(sources[k, 2] + sources[k, 1], sources[k, 0])
    uniform = jnp.max(leaving) + (service[0] + service[1] + sources_top)
    inverse = 1.0 / jnp.full((phases, LANES), uniform, F32)
    scale = jnp.max(inverse)
    wide[...] = jnp.broadcast_to(leaving, (full, LANES))
    exits[...] = wide[rows_here, :] * inverse

    base = lax.axis_index("src") * sh.states
    rates[sh.states, 0] = service[0] * scale
    rates[sh.states, 1] = service[1] * scale
    for s in range(sh.states):
        state = base + s
        feed, outflow, inflow = source_scalars(sources, scale, state)
        rates[s, FEED] = feed
        rates[s, STAY] = 1.0 - feed - outflow
        for k in range(SOURCES):
            rates[s, INFLOW + k] = inflow[k]
        if sh.deferred:
            there = lax.bitwise_xor(state, jnp.int32(1 << sh.bits))
            feed_there, outflow_there, inflow_there = source_scalars(sources, scale, there)
            rates[s, FEED_MORE] = feed_there - feed
            rates[s, STAY_MORE] = (feed + outflow) - (feed_there + outflow_there)
            rates[s, SQUARE] = inflow[sh.bits] * inflow_there[sh.bits]

    for b in range(BATCH + 2):
        if b <= BATCH:
            values = (moving if b == 0 else batch_rates[b - 1]) * scale
            turned[0:full, :] = values
            turned[full:2 * full, :] = values
            turned[0:full, :] = turned[pl.ds(pl.multiple_of(start, phases), full), :].T
            values = turned[rows_here, :]
            high = values.astype(BF16)
            low = (values - high.astype(F32)).astype(BF16)
        else:
            high = jnp.zeros((phases, full), BF16)
            low = high
        parts = (high, low, high)
        for i, part in enumerate(parts):
            if 1 <= b <= BATCH:
                column = ((b - 1) % 2) * 3 * full + i * full
                rim_paired[((b - 1) // 2) * phases:((b - 1) // 2 + 1) * phases, column:column + full] = part
            column = (b % 2) * 3 * full + i * full
            paired[(b // 2) * phases:(b // 2 + 1) * phases, column:column + full] = part


def split(values):
    high = values.astype(BF16)
    low = (values - high.astype(F32)).astype(BF16)
    return [high, high, low]


def inner_kernel(sh, first, spans, plan, rates, weights, exits, own, other, *refs):
    phases = sh.phases
    start_values, raw_got, got_mid = refs[:3] if sh.deferred and not first else (None, None, None)
    out, sent = refs[-2:] if spans[0][0] == "sent" else (refs[-1], None)
    other_at = sh.native if first else sh.by_level
    serve_one, serve_two = rates[sh.states, 0], rates[sh.states, 1]
    lane = lane_ids((phases, LANES))
    inner_one = jnp.where(lane == LANES - 1, 0.0, serve_one)
    later = lane_ids((weights.shape[1] // 6, LANES)) > 0

    def unit_step(group, unit):
        k = lax.div(unit, jnp.int32(sh.states))
        s = unit - k * sh.states
        a, c = plan[k, LEVEL_ONE], plan[k, LEVEL_TWO]
        feed = rates[s, FEED]
        stay = rates[s, STAY] - exits[...] - jnp.where(jnp.logical_or(lane > 0, a > 0), serve_one, 0.0)
        for pair in range(sh.wide_two // 2):
            columns = []
            for u in (2 * pair, 2 * pair + 1):
                values = jnp.concatenate([own[sh.by_level(unit, u), :], other[other_at(unit, u), :]], axis=0)
                columns.append(jnp.concatenate(split(values) + split(jnp.where(later, pltpu.roll(values, 1, 1), 0.0)), axis=0))
            product = jnp.dot(weights[...], jnp.concatenate(columns, axis=1), preferred_element_type=F32)
            for j, u in enumerate((2 * pair, 2 * pair + 1)):
                lanes = slice(j * LANES, (j + 1) * LANES)
                total = product[0:phases, lanes]
                for b in range(1, BATCH // 2 + 1):
                    moved = pltpu.roll(product[b * phases:(b + 1) * phases, lanes], 2 * b, 1)
                    total = total + jnp.where(lane >= 2 * b, moved, 0.0)
                here = own[sh.by_level(unit, u), :]
                two = serve_two if u else jnp.where(c > 0, serve_two, 0.0)
                total = total + (stay - two) * here
                if u:
                    prev = own[sh.by_level(unit, u - 1), :]
                    total = total + inner_one * pltpu.roll(prev, LANES - 1, 1) + feed * prev
                if u + 1 < sh.wide_two:
                    total = total + serve_two * own[sh.by_level(unit, u + 1), :]
                for bit in range(sh.bits):
                    flipped = unit - s + lax.bitwise_xor(s, jnp.int32(1 << bit))
                    total = total + rates[s, INFLOW + bit] * own[sh.by_level(flipped, u), :]
                if start_values is not None:
                    total = total + rates[s, SQUARE] * start_values[sh.by_level(unit, u), :]
                    if group == "raw":
                        more = rates[s, STAY_MORE] * raw_got[sh.by_level(unit, u), :]
                        if u:
                            more = more + rates[s, FEED_MORE] * raw_got[sh.by_level(unit, u - 1), :]
                        total = total + rates[s, INFLOW + sh.bits] * more
                    if group == "mid":
                        total = total + rates[s, INFLOW + sh.bits] * got_mid[sh.by_level(unit - sh.raw_end, u), :]
                out[sh.by_level(unit, u), :] = total
                if group == "sent":
                    more = rates[s, STAY_MORE] * here
                    if u:
                        more = more + rates[s, FEED_MORE] * prev
                    sent[sh.by_level(unit - sh.raw_end, u), :] = 2.0 * total + more

    for group, start, stop in spans:
        sweep(start, stop, 1, functools.partial(unit_step, group))


def halo_kernel(sh, first, *refs):
    refs = list(refs)
    n, phases, last_u = sh.levels, sh.phases, sh.wide_two - 1
    plan, rates = refs[:2]
    refs = refs[2:]
    send_plan = refs.pop(0) if first else None
    weights, inner, own, rims_own, rims_other, columns_own, rim_got, rim_other = refs[:8]
    refs = refs[8:]
    edges, refs = refs[:n - 1], refs[n - 1:]
    raw = 0 if sh.deferred else sh.cross
    partners, refs = refs[:raw], refs[raw:]
    raw_got = refs.pop(0) if sh.deferred and first else None
    out = refs.pop(0)
    sent = refs.pop(0) if sh.deferred and first else None
    rims_out, columns_out = (refs.pop(0), refs.pop(0)) if first else (None, None)
    serve_one, serve_two = rates[sh.states, 0], rates[sh.states, 1]
    lane = lane_ids((phases, LANES))
    group_lane = lax.rem(lane, jnp.int32(BATCH))
    zero = jnp.zeros((phases, LANES), F32)
    if sent is not None:
        for start in range(sh.columns_at, sh.late_rows, phases):
            sent[start:start + phases, :] = zero

    def rim_product(halves):
        columns = []
        for pair in halves:
            values = jnp.concatenate(pair, axis=0)
            ends = lax.rem(lane_ids(values.shape), jnp.int32(BATCH)) == BATCH - 1
            moved = jnp.where(ends, 0.0, pltpu.roll(values, LANES - 1, 1))
            columns.append(jnp.concatenate(split(moved) + split(values), axis=0))
        product = jnp.dot(weights[...], jnp.concatenate(columns, axis=1), preferred_element_type=F32)
        sums = []
        for i in range(len(halves)):
            total = product[(BATCH // 2 - 1) * phases:(BATCH // 2) * phases, i * LANES:(i + 1) * LANES]
            for j in range(BATCH // 2 - 1):
                block = product[j * phases:(j + 1) * phases, i * LANES:(i + 1) * LANES]
                moved = pltpu.roll(block, (2 * j + 2 - BATCH) % LANES, 1)
                total = total + jnp.where(group_lane <= 2 * j + 1, moved, 0.0)
            sums.append(total)
        return sums

    def unit_step(group, unit):
        k = lax.div(unit, jnp.int32(sh.states))
        s = unit - k * sh.states

        def kind(which):
            return plan[k, ROUTES + 3 * which]

        def beside(which):
            return plan[k, ROUTES + 3 * which + 1] + s

        def kept(which):
            return jnp.where(plan[k, ROUTES + 3 * which + 2] > 0, 0.0, 1.0).astype(F32)

        def number(flag):
            return jnp.where(flag, 1.0, 0.0).astype(F32)

        def remote(which, rows):
            value = zero
            for step in range(1, n):
                value = jnp.where(kind(which) == step + 1, edges[step - 1][rows, :], value)
            return value

        small_base = lax.rem(s, jnp.int32(sh.per_small)) * sh.lane_step
        small_at = sh.at(sh.small_rows_at + lax.div(s, jnp.int32(sh.per_small)) * phases)
        edge_at = sh.at(sh.state_rim_rows + unit * phases)
        left = jnp.where(kind(LEFT) == 1, own[sh.by_level(beside(LEFT), last_u), :], remote(LEFT, edge_at))
        right = jnp.where(kind(RIGHT) == 1, own[sh.by_level(beside(RIGHT), 0), :], remote(RIGHT, edge_at))
        above = jnp.where(
            kind(ABOVE) == 1,
            columns_own[sh.at(beside(ABOVE) * phases), :],
            pltpu.roll(remote(ABOVE, small_at), LANES - small_base, 1),
        )
        above = jnp.where(lane < sh.wide_two, above, 0.0) * serve_one
        corner = jnp.where(
            kind(CORNER) == 1,
            pltpu.roll(columns_own[sh.at(beside(CORNER) * phases), :], LANES - 1 - last_u, 1),
            pltpu.roll(remote(CORNER, small_at), LANES - 1 - (small_base + sh.lane_step // 2 + k), 1),
        )
        corner = jnp.where(lane == LANES - 1, corner, 0.0) * serve_one
        shifted = jnp.where(lane == LANES - 1, 0.0, pltpu.roll(left, LANES - 1, 1)) * serve_one
        below_local, below_remote = number(kind(BELOW) == 1), number(kind(BELOW) > 1)
        under = []
        for part in range(sh.rim_parts):
            under.append([
                rims_own[sh.rim_at(beside(BELOW), part), :] * below_local + rim_got[sh.rim_at(s, part), :] * below_remote,
                rims_other[sh.rim_at(beside(BELOW), part), :] * below_local
                + rim_other[sh.rim_at(s, part), :] * below_remote,
            ])
        feed = rates[s, FEED]
        rims = rim_product(under)
        if group is not None:
            keep_left = kept(LEFT)
            rim_scale, column_scale = 2.0 * kept(BELOW), 2.0 * kept(ABOVE)
            sent_first = (2.0 * keep_left) * (shifted + feed * left) + (2.0 * kept(CORNER)) * corner
            sent_first = sent_first + ((2.0 * keep_left - 1.0) * rates[s, FEED_MORE]) * left
            sent_last = (2.0 * kept(RIGHT) * serve_two) * right
            if group != "last":
                sent[sh.at(sh.ends_at + 2 * unit * phases), :] = sent_first
                sent[sh.at(sh.ends_at + (2 * unit + 1) * phases), :] = sent_last
                for part in range(sh.rim_parts):
                    sent[sh.at(sh.rims_at + (unit * sh.rim_parts + part) * phases), :] = rim_scale * rims[part]
                place = sh.at(sh.columns_at + lax.div(unit, jnp.int32(sh.per_column)) * phases)
                base = lax.rem(unit, jnp.int32(sh.per_column)) * sh.wide_two
                sent[place, :] = sent[place, :] + column_scale * pltpu.roll(above, base, 1)
        packed, packed_column = [zero] * sh.rim_parts, zero
        for u in range(sh.wide_two):
            part, q = u // sh.rim_group, u % sh.rim_group

            inside = inner[sh.by_level(unit, u), :]
            rim = jnp.where(lane < BATCH, pltpu.roll(rims[part], LANES - q * BATCH, 1) if q else rims[part], 0.0)
            edge = jnp.where(lane == LANES - 1, pltpu.roll(above, LANES - u, 1), 0.0) if u else zero
            total = inside + rim + edge
            if u == 0:
                total = total + shifted + corner + feed * left
            if u == last_u:
                total = total + serve_two * right
            for bit, values in enumerate(partners):
                total = total + rates[s, INFLOW + sh.bits + bit] * values[sh.by_level(unit, u), :]
            if group == "raw":
                total = total + (2.0 * rates[s, INFLOW + sh.bits]) * raw_got[sh.by_level(unit, u), :]
            if first:
                packed_column = add_packed(sh, lane, packed, packed_column, u, total)
            if first or sh.deferred:
                out[sh.by_level(unit, u), :] = total
            else:
                out[sh.native(unit, u), :] = jnp.where(plan[k, TILE] >= 0, total, 0.0)
            if group == "last":
                value = 2.0 * inside + rim_scale * rim + column_scale * edge
                value = value + rates[s, STAY_MORE] * own[sh.by_level(unit, u), :]
                if u:
                    value = value + rates[s, FEED_MORE] * own[sh.by_level(unit, u - 1), :]
                else:
                    value = value + sent_first
                if u == last_u:
                    value = value + sent_last
                sent[sh.by_level(unit - sh.mid_end, u), :] = value
        if first:
            for part in range(sh.rim_parts):
                rims_out[sh.rim_at(unit, part), :] = packed[part]
            columns_out[sh.at(unit * phases), :] = packed_column

    turn = 2 if first else 4

    if sent is not None:
        sweep(0, sh.raw_end, turn, functools.partial(unit_step, "raw"))
        sweep(sh.raw_end, sh.mid_end, turn, functools.partial(unit_step, "mid"))
        sweep(sh.mid_end, sh.units, turn, functools.partial(unit_step, "last"))
    else:
        sweep(0, sh.units, turn, functools.partial(unit_step, None))
    if first:
        write_messages(sh, send_plan, out, rims_out, columns_out, refs)


def join_kernel(sh, plan, rates, stepped, got_late, out):
    phases, last_u = sh.phases, sh.wide_two - 1
    lane = lane_ids((phases, LANES))
    inflow = rates[0, INFLOW + sh.bits]

    def unit_step(group, unit):
        filled = plan[lax.div(unit, jnp.int32(sh.states)), TILE] >= 0
        if group != "last":
            rims = [
                got_late[sh.at(sh.rims_at + (unit * sh.rim_parts + part) * phases), :] for part in range(sh.rim_parts)
            ]
            column = got_late[sh.at(sh.columns_at + lax.div(unit, jnp.int32(sh.per_column)) * phases), :]
            base = lax.rem(unit, jnp.int32(sh.per_column)) * sh.wide_two
        for u in range(sh.wide_two):
            if group == "last":
                got = got_late[sh.by_level(unit - sh.mid_end, u), :]
            else:
                part, q = u // sh.rim_group, u % sh.rim_group
                got = jnp.where(lane < BATCH, pltpu.roll(rims[part], LANES - q * BATCH, 1) if q else rims[part], 0.0)
                if u:
                    got = jnp.where(lane == LANES - 1, pltpu.roll(column, LANES - (base + u), 1), got)
                if u in (0, last_u):
                    got = got + got_late[sh.at(sh.ends_at + (2 * unit + (1 if u else 0)) * phases), :]
            total = stepped[sh.by_level(unit, u), :] + inflow * got
            out[sh.native(unit, u), :] = jnp.where(filled, total, 0.0)

    sweep(0, sh.mid_end, JOIN_TURN, functools.partial(unit_step, None))
    sweep(sh.mid_end, sh.units, JOIN_TURN, functools.partial(unit_step, "last"))


def body(
    state_values,
    phase_rates,
    batch_rates,
    service_rates,
    source_rates,
    tile_levels,
    routes,
    tile_owner,
):
    block = state_values.shape
    sh = Shape(block, tile_owner.shape[0], lax.axis_size("level"))
    n, full = sh.levels, phase_rates.shape[0]
    flat = state_values.reshape(sh.rows, LANES)
    smem, vmem = pl.BlockSpec(memory_space=SM), pl.BlockSpec(memory_space=VM)

    def array(rows):
        return jax.ShapeDtypeStruct((rows, LANES), F32)

    def table(rows, columns, dtype=F32):
        return jax.ShapeDtypeStruct((rows, columns), dtype)

    def call(kernel, scalars, arrays, shapes, micros, scalar_shapes=(), scratch=(), space=VM, aliases=None):
        return pl.pallas_call(
            kernel,
            out_shape=tuple(scalar_shapes) + tuple(shapes),
            in_specs=[smem] * len(scalars) + [pl.BlockSpec(memory_space=space)] * len(arrays),
            out_specs=tuple([smem] * len(scalar_shapes) + [vmem] * len(shapes)),
            scratch_shapes=list(scratch),
            input_output_aliases=aliases or {},
            cost_estimate=pl.CostEstimate(flops=0, bytes_accessed=int(micros * 3.0e6), transcendentals=0),
            compiler_params=pltpu.CompilerParams(vmem_limit_bytes=GRANT),
        )(*scalars, *arrays)

    packed_shapes = [array(sh.rim_rows), array(sh.edge_rows)] + [array(sh.message_rows)] * (n - 1)

    def along_level(x, step):
        return permute(x, "level", lambda i: sh.sends_to(i, step))

    def exchange(messages, inside):
        got = []
        for i in range(n - 1):
            got.append(along_level(messages[i], i + 1))
        got, inside = lax.optimization_barrier((got, inside))
        rim_got = sum(values[:sh.state_rim_rows] for values in got)
        return [rim_got, from_next(rim_got, "phase")] + got, inside

    other = from_next(flat, "phase")

    def in_hbm(values):
        return [pltpu.with_memory_space_constraint(v, pltpu.HBM) for v in values]

    routes, tile_owner, flat = in_hbm([routes, tile_owner, flat])
    send_plan, *outs = call(
        functools.partial(pack_kernel, sh),
        [routes, tile_owner],
        [flat],
        ([array(sh.raw_rows)] if sh.deferred else []) + [array(sh.rows)] + packed_shapes,
        3,
        [table(n - 1, PICKS + 2 * sh.slots, I32)],
        [VM((sh.rows, LANES), F32), pltpu.SemaphoreType.DMA((sh.slots,))],
        pltpu.HBM,
    )
    if sh.deferred:
        raw_got, outs = from_partner(outs[0], "src", 0), outs[1:]
    start, rims, columns, messages = outs[0], outs[1], outs[2], outs[3:]
    plan, rates, paired, rim_paired, exits = call(
        functools.partial(prep_kernel, sh),
        [routes, tile_owner, *in_hbm([tile_levels.T, service_rates, source_rates])],
        in_hbm([phase_rates, batch_rates]),
        [
            table((BATCH // 2 + 1) * sh.phases, 6 * full, BF16),
            table((BATCH // 2) * sh.phases, 6 * full, BF16),
            array(sh.phases),
        ],
        2,
        [table(sh.slots, ROUTES + 15, I32), table(sh.states + 1, INFLOW + SOURCES)],
        [VM((2 * full, full), F32), VM((full, LANES), F32)],
    )

    def inner(first, values, other, spans, extra=(), aliases=None):
        shapes = [array(sh.rows)]
        if spans[0][0] == "sent":
            shapes.append(array(sh.mid_rows))
        operands = [paired, exits, values, other, *extra]
        micros = 9 * sum(stop - start for _, start, stop in spans) / sh.units
        kernel = functools.partial(inner_kernel, sh, first, spans)
        return call(kernel, [plan, rates], operands, shapes, micros, aliases=aliases)

    def halo(first, inside, values, rims, columns, got, extra):
        shapes = [array(sh.rows)]
        if first:
            shapes += ([array(sh.late_rows)] if sh.deferred else []) + packed_shapes
        rims_other = from_next(rims, "phase")
        return call(
            functools.partial(halo_kernel, sh, first),
            [plan, rates] + ([send_plan] if first else []),
            [rim_paired, inside, values, rims, rims_other, columns] + got + extra,
            shapes,
            4,
        )

    if sh.deferred:
        inside, mid = inner(True, start, other, [("sent", sh.raw_end, sh.mid_end)])
        got_mid = from_partner(mid, "src", 0)
        spans = [(None, 0, sh.raw_end), (None, sh.mid_end, sh.units)]
        (inside,) = inner(True, start, other, spans, [inside], {6: 0})
        got, inside = exchange(messages, inside)
        outs = halo(True, inside, start, rims, columns, got, [raw_got])
        once, late, rims, columns, messages = outs[0], outs[1], outs[2], outs[3], outs[4:]
        got_late = from_partner(late, "src", 0)
        other = from_next(once, "phase")
        (inside,) = inner(
            False,
            once,
            other,
            [("raw", 0, sh.raw_end), ("mid", sh.raw_end, sh.mid_end), (None, sh.mid_end, sh.units)],
            [start, raw_got, got_mid],
        )
        got, inside = exchange(messages, inside)
        (twice,) = halo(False, inside, once, rims, columns, got, [])
        (result,) = call(
            functools.partial(join_kernel, sh), [plan, rates], [twice, got_late], [array(sh.rows)], 3
        )
    else:
        (inside,) = inner(True, start, other, [(None, 0, sh.units)])
        got, inside = exchange(messages, inside)
        extra = [from_partner(start, "src", bit) for bit in range(sh.cross)]
        outs = halo(True, inside, start, rims, columns, got, extra)
        once, rims, columns, messages = outs[0], outs[1], outs[2], outs[3:]
        (inside,) = inner(False, once, from_next(once, "phase"), [(None, 0, sh.units)])
        got, inside = exchange(messages, inside)
        extra = [from_partner(once, "src", bit) for bit in range(sh.cross)]
        (result,) = halo(False, inside, once, rims, columns, got, extra)
    return result.reshape(block)


def solution(mesh):
    placed = (
        P(("groups", "level"), "src", "phase", None, None),
        P("groups", None),
        P("groups", None, None),
        P("groups"),
        P("groups", None),
        P("groups", None),
        P("groups", None),
        P("groups"),
    )

    return jax.shard_map(
        body,
        mesh=mesh,
        in_specs=placed,
        out_specs=P(("groups", "level"), "src", "phase", None, None),
        check_vma=False,
    )
```

```python
import functools

import jax
import jax.numpy as jnp
from jax import lax
from jax.experimental import pallas as pl
from jax.experimental.pallas import tpu as pltpu
from jax.sharding import PartitionSpec as P


BATCH = 16
SOURCES = 3
LANES = 128
F32 = jnp.float32
BF16 = jnp.bfloat16
I32 = jnp.int32
VM = pltpu.VMEM
SM = pltpu.SMEM
GRANT = 24 << 20
PACK_TURN = 4

FEED, STAY, FEED_MORE, STAY_MORE, SQUARE, INFLOW = 0, 1, 2, 3, 4, 5
TILE, LEVEL_ONE, LEVEL_TWO, ROUTES = 0, 1, 2, 3
BELOW, ABOVE, LEFT, RIGHT, CORNER = 0, 1, 2, 3, 4
ROW, WANTED, LAST, PICKS = 0, 1, 2, 3


def permute(x, axis, pairs_of):
    return lax.ppermute(x, axis, [(i, pairs_of(i)) for i in range(lax.axis_size(axis))])


def from_next(x, axis):
    n = lax.axis_size(axis)
    return permute(x, axis, lambda i: (i - 1) % n)


def from_partner(x, axis, bit):
    return permute(x, axis, lambda i: i ^ 1 << bit)


class Shape:
    def __init__(self, block, tiles, levels):
        self.slots, self.states, self.phases, self.wide_two, self.wide_one = block
        self.tiles = tiles
        self.levels = levels
        self.units = self.slots * self.states
        self.rows = self.units * self.phases * self.wide_two
        self.rim_group = LANES // BATCH
        self.rim_parts = self.wide_two // self.rim_group
        self.state_rim_rows = self.states * self.rim_parts * self.phases
        self.rim_rows = self.slots * self.state_rim_rows
        self.edge_rows = self.units * self.phases
        self.lane_step = 2 * max(self.wide_two, BATCH)
        self.per_small = LANES // self.lane_step
        self.small_blocks = -(-self.states // self.per_small)
        self.small_rows_at = self.state_rim_rows + self.edge_rows
        self.message_rows = self.small_rows_at + self.small_blocks * self.phases
        self.bits = self.states.bit_length() - 1
        self.cross = SOURCES - self.bits
        self.deferred = self.cross == 1
        self.raw_end = self.states
        self.mid_end = self.units - self.states
        self.raw_rows = self.raw_end * self.wide_two * self.phases
        self.mid_rows = (self.mid_end - self.raw_end) * self.wide_two * self.phases
        self.ends_at = self.states * self.wide_two * self.phases
        self.rims_at = self.ends_at + self.mid_end * 2 * self.phases
        self.rim_units = max(self.mid_end - self.states, self.raw_end)
        self.columns_at = self.rims_at + self.rim_units * self.rim_parts * self.phases
        self.per_column = LANES // self.wide_two
        self.late_rows = self.columns_at + -(-self.mid_end // self.per_column) * self.phases
        self.power = levels & (levels - 1) == 0

    def at(self, start):
        if not isinstance(start, int):
            start = pl.multiple_of(start, self.phases)
        return pl.ds(start, self.phases)

    def native(self, unit, u):
        return pl.ds(unit * self.phases * self.wide_two + u, self.phases, stride=self.wide_two)

    def by_level(self, unit, u):
        return self.at((unit * self.wide_two + u) * self.phases)

    def rim_at(self, unit, part):
        return self.at((unit * self.rim_parts + part) * self.phases)

    def sent_rim_at(self, unit, part):
        index = unit if isinstance(unit, int) else jnp.where(unit < self.raw_end, unit, unit - self.states)
        return self.at(self.rims_at + (index * self.rim_parts + part) * self.phases)

    def small_at(self, state):
        return state // self.per_small, (state % self.per_small) * self.lane_step

    def sends_to(self, me, step):
        return me ^ step if self.power else (me + step) % self.levels

    def takes_from(self, me, step):
        return me ^ step if self.power else (me + self.levels - step) % self.levels


def sweep(start, stop, wished, visit):
    many = wished if (stop - start) % wished == 0 else 1

    def turn(index, carry):
        for j in range(many):
            visit(start + index * many + j)
        return carry

    lax.fori_loop(0, (stop - start) // many, turn, 0)


def lane_ids(shape):
    return lax.broadcasted_iota(I32, shape, len(shape) - 1)


def tile_at(owner, slot, tiles):
    found = jnp.int32(-1)
    for t in range(tiles):
        found = jnp.where(owner[t] == slot, t, found)
    return found


def route_of(routes, owner, tile, direction, slots):
    known = jnp.maximum(tile, 0)
    target = jnp.where(tile >= 0, routes[known, direction], -1)
    slot = owner[jnp.maximum(target, 0)]
    device = lax.div(slot, jnp.int32(slots))
    return target >= 0, device, slot - device * slots


def peer(sh, me, step, sending):
    if sh.power:
        return lax.bitwise_xor(me, jnp.int32(step))
    return lax.rem(me + (step if sending else sh.levels - step), jnp.int32(sh.levels))


def fill_send_plan(sh, routes, owner, plan):
    me = lax.axis_index("level")
    first = tile_at(owner, me * sh.slots, sh.tiles)
    count = jnp.int32(0)
    for k in range(sh.slots):
        count = count + jnp.where(tile_at(owner, me * sh.slots + k, sh.tiles) >= 0, 1, 0)
    for step in range(1, sh.levels):
        there = peer(sh, me, step, True)
        their_first = tile_at(owner, there * sh.slots, sh.tiles)
        lower = first < their_first
        found, device, _ = route_of(routes, owner, their_first, BELOW, sh.slots)
        plan[step - 1, ROW] = jnp.where(lower, sh.wide_two - 1, 0)
        plan[step - 1, WANTED] = jnp.where(jnp.logical_and(found, device == me), 1, 0)
        plan[step - 1, LAST] = (count - 1) * sh.states
        for k in range(sh.slots):
            tile = tile_at(owner, there * sh.slots + k, sh.tiles)
            _, _, left = route_of(routes, owner, tile, LEFT, sh.slots)
            _, _, right = route_of(routes, owner, tile, RIGHT, sh.slots)
            _, _, corner = route_of(routes, owner, tile, CORNER, sh.slots)
            plan[step - 1, PICKS + 2 * k] = jnp.where(lower, left, right) * sh.states
            plan[step - 1, PICKS + 2 * k + 1] = corner * sh.states


def add_packed(sh, lane, rims, column, u, values):
    part, q = u // sh.rim_group, u % sh.rim_group
    moved = pltpu.roll(values, (q * BATCH - (sh.wide_one - BATCH)) % LANES, 1)
    rims[part] = jnp.where(lax.div(lane, jnp.int32(BATCH)) == q, moved, rims[part])
    moved = pltpu.roll(values, u, 1) if u else values
    return jnp.where(lane == u, moved, column)


def write_messages(sh, plan, data, rims, columns, messages):
    phases, last_u = sh.phases, sh.wide_two - 1
    lane = lane_ids((phases, LANES))
    bottoms = [jnp.zeros((phases, LANES), F32) for _ in range(sh.small_blocks)]
    for s in range(sh.states):
        block, base = sh.small_at(s)
        values = columns[sh.at(s * phases), :]
        bottoms[block] = bottoms[block] + (pltpu.roll(values, base, 1) if base else values)
    for step in range(1, sh.levels):
        row = plan[step - 1, ROW]
        wanted = jnp.where(plan[step - 1, WANTED] > 0, 1.0, 0.0).astype(F32)
        last = plan[step - 1, LAST]
        for s in range(sh.states):
            for part in range(sh.rim_parts):
                messages[step - 1][sh.rim_at(s, part), :] = rims[sh.rim_at(last + s, part), :] * wanted
        small = list(bottoms)
        for k in range(sh.slots):
            slot, corner = plan[step - 1, PICKS + 2 * k], plan[step - 1, PICKS + 2 * k + 1]
            for s in range(sh.states):
                messages[step - 1][sh.at(sh.state_rim_rows + (k * sh.states + s) * phases), :] = data[sh.by_level(slot + s, row), :]
                block, base = sh.small_at(s)
                place = base + sh.lane_step // 2 + k
                moved = pltpu.roll(columns[sh.at((corner + s) * phases), :], (place - last_u) % LANES, 1)
                small[block] = jnp.where(lane == place, moved, small[block])
        for i, values in enumerate(small):
            messages[step - 1][sh.at(sh.small_rows_at + i * phases), :] = values


def pack_kernel(sh, routes, owner, data_hbm, send_plan, *outs):
    outs, (data, arrived) = outs[:-2], outs[-2:]
    raw, (by_level, rims, columns, *messages) = (outs[0], outs[1:]) if sh.deferred else (None, outs)
    lane = lane_ids((sh.phases, LANES))
    size = sh.rows // sh.slots
    copies = [
        pltpu.make_async_copy(data_hbm.at[pl.ds(k * size, size)], data.at[pl.ds(k * size, size)], arrived.at[k])
        for k in range(sh.slots)
    ]
    for copy in copies:
        copy.start()
    fill_send_plan(sh, routes, owner, send_plan)

    def reorder(to_src, unit):
        packed = [jnp.zeros((sh.phases, LANES), F32) for _ in range(sh.rim_parts)]
        column = jnp.zeros((sh.phases, LANES), F32)
        for u in range(sh.wide_two):
            values = data[sh.native(unit, u), :]
            by_level[sh.by_level(unit, u), :] = values
            if to_src:
                raw[sh.by_level(unit, u), :] = values
            column = add_packed(sh, lane, packed, column, u, values)
        for part, values in enumerate(packed):
            rims[sh.rim_at(unit, part), :] = values
        columns[sh.at(unit * sh.phases), :] = column

    for k, copy in enumerate(copies):
        copy.wait()
        sweep(k * sh.states, (k + 1) * sh.states, PACK_TURN, functools.partial(reorder, sh.deferred and k == 0))
    write_messages(sh, send_plan, by_level, rims, columns, messages)


def source_scalars(sources, scale, state):
    feed = jnp.float32(0.0)
    outflow = jnp.float32(0.0)
    inflow = []
    for k in range(SOURCES):
        on = lax.rem(lax.shift_right_logical(state, jnp.int32(k)), jnp.int32(2)) == 1
        turn_on, turn_off, arrive = sources[k, 0], sources[k, 1], sources[k, 2]
        feed = feed + jnp.where(on, arrive, 0.0)
        outflow = outflow + jnp.where(on, turn_off, turn_on)
        inflow.append(jnp.where(on, turn_on, turn_off) * scale)
    return feed * scale, outflow * scale, inflow


def prep_kernel(sh, routes, owner, levels_t, service, sources, phase_rates, batch_rates, plan, rates, paired, rim_paired,
                exits, turned, wide):
    me = lax.axis_index("level")
    for k in range(sh.slots):
        tile = tile_at(owner, me * sh.slots + k, sh.tiles)
        known = jnp.maximum(tile, 0)
        plan[k, TILE] = tile
        plan[k, LEVEL_ONE] = levels_t[0, known]
        plan[k, LEVEL_TWO] = levels_t[1, known]
        for r in range(5):
            found, device, slot = route_of(routes, owner, tile, r, sh.slots)
            kind = jnp.int32(1)
            for step in range(1, sh.levels):
                kind = jnp.where(device == peer(sh, me, step, False), step + 1, kind)
            plan[k, ROUTES + 3 * r] = jnp.where(found, kind, 0)
            plan[k, ROUTES + 3 * r + 1] = slot * sh.states
            plan[k, ROUTES + 3 * r + 2] = jnp.where(slot == 0, 1, 0)

    phases, full = sh.phases, phase_rates.shape[0]
    start = lax.axis_index("phase") * phases
    rows_here = pl.ds(pl.multiple_of(start, phases), phases)
    shape = (full, full)
    moving = phase_rates[...]
    moving = jnp.where(lax.broadcasted_iota(I32, shape, 0) == lax.broadcasted_iota(I32, shape, 1), 0.0, moving)
    total = moving
    for b in range(BATCH):
        total = total + batch_rates[b]
    leaving = jnp.sum(total, axis=1, keepdims=True)
    sources_top = jnp.float32(0.0)
    for k in range(SOURCES):
        sources_top = sources_top + jnp.maximum(sources[k, 2] + sources[k, 1], sources[k, 0])
    uniform = jnp.max(leaving) + (service[0] + service[1] + sources_top)
    inverse = 1.0 / jnp.full((phases, LANES), uniform, F32)
    scale = jnp.max(inverse)
    wide[...] = jnp.broadcast_to(leaving, (full, LANES))
    exits[...] = wide[rows_here, :] * inverse

    base = lax.axis_index("src") * sh.states
    rates[sh.states, 0] = service[0] * scale
    rates[sh.states, 1] = service[1] * scale
    for s in range(sh.states):
        state = base + s
        feed, outflow, inflow = source_scalars(sources, scale, state)
        rates[s, FEED] = feed
        rates[s, STAY] = 1.0 - feed - outflow
        for k in range(SOURCES):
            rates[s, INFLOW + k] = inflow[k]
        if sh.deferred:
            there = lax.bitwise_xor(state, jnp.int32(1 << sh.bits))
            feed_there, outflow_there, inflow_there = source_scalars(sources, scale, there)
            rates[s, FEED_MORE] = feed_there - feed
            rates[s, STAY_MORE] = (feed + outflow) - (feed_there + outflow_there)
            rates[s, SQUARE] = inflow[sh.bits] * inflow_there[sh.bits]

    for b in range(BATCH + 2):
        if b <= BATCH:
            values = (moving if b == 0 else batch_rates[b - 1]) * scale
            turned[0:full, :] = values
            turned[full:2 * full, :] = values
            turned[0:full, :] = turned[pl.ds(pl.multiple_of(start, phases), full), :].T
            values = turned[rows_here, :]
            high = values.astype(BF16)
            low = (values - high.astype(F32)).astype(BF16)
        else:
            high = jnp.zeros((phases, full), BF16)
            low = high
        parts = (high, low, high)
        for i, part in enumerate(parts):
            if 1 <= b <= BATCH:
                column = ((b - 1) % 2) * 3 * full + i * full
                rim_paired[((b - 1) // 2) * phases:((b - 1) // 2 + 1) * phases, column:column + full] = part
            column = (b % 2) * 3 * full + i * full
            paired[(b // 2) * phases:(b // 2 + 1) * phases, column:column + full] = part


def split(values):
    high = values.astype(BF16)
    low = (values - high.astype(F32)).astype(BF16)
    return [high, high, low]


def inner_kernel(sh, first, spans, plan, rates, weights, exits, own, other, *refs):
    phases = sh.phases
    start_values, raw_got, got_mid = refs[:3] if sh.deferred and not first else (None, None, None)
    out, sent = refs[-2:] if spans[0][0] == "sent" else (refs[-1], None)
    other_at = sh.native if first else sh.by_level
    serve_one, serve_two = rates[sh.states, 0], rates[sh.states, 1]
    lane = lane_ids((phases, LANES))
    inner_one = jnp.where(lane == LANES - 1, 0.0, serve_one)
    later = lane_ids((weights.shape[1] // 6, LANES)) > 0

    def unit_step(group, unit):
        k = lax.div(unit, jnp.int32(sh.states))
        s = unit - k * sh.states
        a, c = plan[k, LEVEL_ONE], plan[k, LEVEL_TWO]
        feed = rates[s, FEED]
        stay = rates[s, STAY] - exits[...] - jnp.where(jnp.logical_or(lane > 0, a > 0), serve_one, 0.0)
        for pair in range(sh.wide_two // 2):
            columns = []
            for u in (2 * pair, 2 * pair + 1):
                values = jnp.concatenate([own[sh.by_level(unit, u), :], other[other_at(unit, u), :]], axis=0)
                columns.append(jnp.concatenate(split(values) + split(jnp.where(later, pltpu.roll(values, 1, 1), 0.0)), axis=0))
            product = jnp.dot(weights[...], jnp.concatenate(columns, axis=1), preferred_element_type=F32)
            for j, u in enumerate((2 * pair, 2 * pair + 1)):
                lanes = slice(j * LANES, (j + 1) * LANES)
                total = product[0:phases, lanes]
                for b in range(1, BATCH // 2 + 1):
                    moved = pltpu.roll(product[b * phases:(b + 1) * phases, lanes], 2 * b, 1)
                    total = total + jnp.where(lane >= 2 * b, moved, 0.0)
                here = own[sh.by_level(unit, u), :]
                two = serve_two if u else jnp.where(c > 0, serve_two, 0.0)
                total = total + (stay - two) * here
                if u:
                    prev = own[sh.by_level(unit, u - 1), :]
                    total = total + inner_one * pltpu.roll(prev, LANES - 1, 1) + feed * prev
                if u + 1 < sh.wide_two:
                    total = total + serve_two * own[sh.by_level(unit, u + 1), :]
                for bit in range(sh.bits):
                    flipped = unit - s + lax.bitwise_xor(s, jnp.int32(1 << bit))
                    total = total + rates[s, INFLOW + bit] * own[sh.by_level(flipped, u), :]
                if start_values is not None:
                    total = total + rates[s, SQUARE] * start_values[sh.by_level(unit, u), :]
                    if group == "raw":
                        more = rates[s, STAY_MORE] * raw_got[sh.by_level(unit, u), :]
                        if u:
                            more = more + rates[s, FEED_MORE] * raw_got[sh.by_level(unit, u - 1), :]
                        total = total + rates[s, INFLOW + sh.bits] * more
                    if group == "mid":
                        total = total + rates[s, INFLOW + sh.bits] * got_mid[sh.by_level(unit - sh.raw_end, u), :]
                out[sh.by_level(unit, u), :] = total
                if group == "sent":
                    more = rates[s, STAY_MORE] * here
                    if u:
                        more = more + rates[s, FEED_MORE] * prev
                    sent[sh.by_level(unit - sh.raw_end, u), :] = 2.0 * total + more

    for group, start, stop in spans:
        sweep(start, stop, 1, functools.partial(unit_step, group))


def halo_kernel(sh, first, *refs):
    refs = list(refs)
    n, phases, last_u = sh.levels, sh.phases, sh.wide_two - 1
    plan, rates = refs[:2]
    refs = refs[2:]
    send_plan = refs.pop(0) if first else None
    weights, inner, own, rims_own, rims_other, columns_own, rim_got, rim_other = refs[:8]
    refs = refs[8:]
    edges, refs = refs[:n - 1], refs[n - 1:]
    raw = 0 if sh.deferred else sh.cross
    partners, refs = refs[:raw], refs[raw:]
    raw_got = refs.pop(0) if sh.deferred and first else None
    out = refs.pop(0)
    sent = refs.pop(0) if sh.deferred and first else None
    rims_out, columns_out = (refs.pop(0), refs.pop(0)) if first else (None, None)
    serve_one, serve_two = rates[sh.states, 0], rates[sh.states, 1]
    lane = lane_ids((phases, LANES))
    group_lane = lax.rem(lane, jnp.int32(BATCH))
    zero = jnp.zeros((phases, LANES), F32)
    if sent is not None:
        for start in range(sh.columns_at, sh.late_rows, phases):
            sent[start:start + phases, :] = zero

    def rim_product(halves):
        columns = []
        for pair in halves:
            values = jnp.concatenate(pair, axis=0)
            ends = lax.rem(lane_ids(values.shape), jnp.int32(BATCH)) == BATCH - 1
            moved = jnp.where(ends, 0.0, pltpu.roll(values, LANES - 1, 1))
            columns.append(jnp.concatenate(split(moved) + split(values), axis=0))
        product = jnp.dot(weights[...], jnp.concatenate(columns, axis=1), preferred_element_type=F32)
        sums = []
        for i in range(len(halves)):
            total = product[(BATCH // 2 - 1) * phases:(BATCH // 2) * phases, i * LANES:(i + 1) * LANES]
            for j in range(BATCH // 2 - 1):
                block = product[j * phases:(j + 1) * phases, i * LANES:(i + 1) * LANES]
                moved = pltpu.roll(block, (2 * j + 2 - BATCH) % LANES, 1)
                total = total + jnp.where(group_lane <= 2 * j + 1, moved, 0.0)
            sums.append(total)
        return sums

    def unit_step(group, unit):
        k = lax.div(unit, jnp.int32(sh.states))
        s = unit - k * sh.states

        def kind(which):
            return plan[k, ROUTES + 3 * which]

        def beside(which):
            return plan[k, ROUTES + 3 * which + 1] + s

        def kept(which):
            return jnp.where(plan[k, ROUTES + 3 * which + 2] > 0, 0.0, 1.0).astype(F32)

        def number(flag):
            return jnp.where(flag, 1.0, 0.0).astype(F32)

        def remote(which, rows):
            value = zero
            for step in range(1, n):
                value = jnp.where(kind(which) == step + 1, edges[step - 1][rows, :], value)
            return value

        small_base = lax.rem(s, jnp.int32(sh.per_small)) * sh.lane_step
        small_at = sh.at(sh.small_rows_at + lax.div(s, jnp.int32(sh.per_small)) * phases)
        edge_at = sh.at(sh.state_rim_rows + unit * phases)
        left = jnp.where(kind(LEFT) == 1, own[sh.by_level(beside(LEFT), last_u), :], remote(LEFT, edge_at))
        right = jnp.where(kind(RIGHT) == 1, own[sh.by_level(beside(RIGHT), 0), :], remote(RIGHT, edge_at))
        above = jnp.where(
            kind(ABOVE) == 1,
            columns_own[sh.at(beside(ABOVE) * phases), :],
            pltpu.roll(remote(ABOVE, small_at), LANES - small_base, 1),
        )
        above = jnp.where(lane < sh.wide_two, above, 0.0) * serve_one
        corner = jnp.where(
            kind(CORNER) == 1,
            pltpu.roll(columns_own[sh.at(beside(CORNER) * phases), :], LANES - 1 - last_u, 1),
            pltpu.roll(remote(CORNER, small_at), LANES - 1 - (small_base + sh.lane_step // 2 + k), 1),
        )
        corner = jnp.where(lane == LANES - 1, corner, 0.0) * serve_one
        shifted = jnp.where(lane == LANES - 1, 0.0, pltpu.roll(left, LANES - 1, 1)) * serve_one
        below_local, below_remote = number(kind(BELOW) == 1), number(kind(BELOW) > 1)
        under = []
        for part in range(sh.rim_parts):
            under.append([
                rims_own[sh.rim_at(beside(BELOW), part), :] * below_local + rim_got[sh.rim_at(s, part), :] * below_remote,
                rims_other[sh.rim_at(beside(BELOW), part), :] * below_local
                + rim_other[sh.rim_at(s, part), :] * below_remote,
            ])
        feed = rates[s, FEED]
        rims = rim_product(under)
        if group is not None:
            keep_left = kept(LEFT)
            rim_scale, column_scale = 2.0 * kept(BELOW), 2.0 * kept(ABOVE)
            sent_first = (2.0 * keep_left) * (shifted + feed * left) + (2.0 * kept(CORNER)) * corner
            sent_first = sent_first + ((2.0 * keep_left - 1.0) * rates[s, FEED_MORE]) * left
            sent_last = (2.0 * kept(RIGHT) * serve_two) * right
            if group != "last":
                sent[sh.at(sh.ends_at + 2 * unit * phases), :] = sent_first
                sent[sh.at(sh.ends_at + (2 * unit + 1) * phases), :] = sent_last
                if group != "second":
                    for part in range(sh.rim_parts):
                        sent[sh.sent_rim_at(unit, part), :] = rim_scale * rims[part]
                place = sh.at(sh.columns_at + lax.div(unit, jnp.int32(sh.per_column)) * phases)
                base = lax.rem(unit, jnp.int32(sh.per_column)) * sh.wide_two
                sent[place, :] = sent[place, :] + column_scale * pltpu.roll(above, base, 1)
        packed, packed_column = [zero] * sh.rim_parts, zero
        for u in range(sh.wide_two):
            part, q = u // sh.rim_group, u % sh.rim_group

            inside = inner[sh.by_level(unit, u), :]
            rim = jnp.where(lane < BATCH, pltpu.roll(rims[part], LANES - q * BATCH, 1) if q else rims[part], 0.0)
            edge = jnp.where(lane == LANES - 1, pltpu.roll(above, LANES - u, 1), 0.0) if u else zero
            total = inside + rim + edge
            if u == 0:
                total = total + shifted + corner + feed * left
            if u == last_u:
                total = total + serve_two * right
            for bit, values in enumerate(partners):
                total = total + rates[s, INFLOW + sh.bits + bit] * values[sh.by_level(unit, u), :]
            if group == "raw":
                total = total + (2.0 * rates[s, INFLOW + sh.bits]) * raw_got[sh.by_level(unit, u), :]
            if first:
                packed_column = add_packed(sh, lane, packed, packed_column, u, total)
            if first or sh.deferred:
                out[sh.by_level(unit, u), :] = total
            else:
                out[sh.native(unit, u), :] = jnp.where(plan[k, TILE] >= 0, total, 0.0)
            if group == "last":
                value = 2.0 * inside + rim_scale * rim + column_scale * edge
                value = value + rates[s, STAY_MORE] * own[sh.by_level(unit, u), :]
                if u:
                    value = value + rates[s, FEED_MORE] * own[sh.by_level(unit, u - 1), :]
                else:
                    value = value + sent_first
                if u == last_u:
                    value = value + sent_last
                sent[sh.by_level(unit - sh.mid_end, u), :] = value
        if first:
            for part in range(sh.rim_parts):
                rims_out[sh.rim_at(unit, part), :] = packed[part]
            columns_out[sh.at(unit * phases), :] = packed_column

    turn = 2 if first else 4

    if sent is not None:
        sweep(0, sh.raw_end, turn, functools.partial(unit_step, "raw"))
        second_end = min(2 * sh.states, sh.mid_end)
        sweep(sh.raw_end, second_end, turn, functools.partial(unit_step, "second"))
        if sh.mid_end > second_end:
            sweep(second_end, sh.mid_end, turn, functools.partial(unit_step, "mid"))
        sweep(sh.mid_end, sh.units, turn, functools.partial(unit_step, "last"))
    else:
        sweep(0, sh.units, turn, functools.partial(unit_step, None))
    if first:
        write_messages(sh, send_plan, out, rims_out, columns_out, refs)


def join_kernel(sh, plan, rates, stepped, got_late, out):
    phases, last_u = sh.phases, sh.wide_two - 1
    lane = lane_ids((phases, LANES))
    inflow = rates[0, INFLOW + sh.bits]
    slot = pl.program_id(0)
    filled = plan[slot, TILE] >= 0

    def unit_step(group, state):
        unit = slot * sh.states + state
        if group != "last":
            column = got_late[sh.at(sh.columns_at + lax.div(unit, jnp.int32(sh.per_column)) * phases), :]
            base = lax.rem(unit, jnp.int32(sh.per_column)) * sh.wide_two
        if group == "rims":
            rims = [got_late[sh.sent_rim_at(unit, part), :] for part in range(sh.rim_parts)]
        for u in range(sh.wide_two):
            if group == "last":
                got = got_late[sh.by_level(unit - sh.mid_end, u), :]
            else:
                got = jnp.zeros((phases, LANES), F32)
                if group == "rims":
                    part, q = u // sh.rim_group, u % sh.rim_group
                    got = jnp.where(lane < BATCH, pltpu.roll(rims[part], LANES - q * BATCH, 1) if q else rims[part], 0.0)
                if u:
                    got = jnp.where(lane == LANES - 1, pltpu.roll(column, LANES - (base + u), 1), got)
                if u in (0, last_u):
                    got = got + got_late[sh.at(sh.ends_at + (2 * unit + (1 if u else 0)) * phases), :]
            total = stepped[sh.by_level(unit, u), :] + inflow * got
            out[sh.native(state, u), :] = jnp.where(filled, total, 0.0)

    def slot_step(group):
        sweep(0, sh.states, 4, functools.partial(unit_step, group))

    last = slot == sh.slots - 1
    second = jnp.logical_and(slot == 1, jnp.logical_not(last))
    pl.when(last)(functools.partial(slot_step, "last"))
    pl.when(second)(functools.partial(slot_step, "second"))
    pl.when(jnp.logical_not(jnp.logical_or(last, second)))(functools.partial(slot_step, "rims"))


def body(
    state_values,
    phase_rates,
    batch_rates,
    service_rates,
    source_rates,
    tile_levels,
    routes,
    tile_owner,
):
    block = state_values.shape
    sh = Shape(block, tile_owner.shape[0], lax.axis_size("level"))
    n, full = sh.levels, phase_rates.shape[0]
    flat = state_values.reshape(sh.rows, LANES)
    smem, vmem = pl.BlockSpec(memory_space=SM), pl.BlockSpec(memory_space=VM)

    def array(rows):
        return jax.ShapeDtypeStruct((rows, LANES), F32)

    def table(rows, columns, dtype=F32):
        return jax.ShapeDtypeStruct((rows, columns), dtype)

    def call(kernel, scalars, arrays, shapes, micros, scalar_shapes=(), scratch=(), space=VM, aliases=None):
        return pl.pallas_call(
            kernel,
            out_shape=tuple(scalar_shapes) + tuple(shapes),
            in_specs=[smem] * len(scalars) + [pl.BlockSpec(memory_space=space)] * len(arrays),
            out_specs=tuple([smem] * len(scalar_shapes) + [vmem] * len(shapes)),
            scratch_shapes=list(scratch),
            input_output_aliases=aliases or {},
            cost_estimate=pl.CostEstimate(flops=0, bytes_accessed=int(micros * 3.0e6), transcendentals=0),
            compiler_params=pltpu.CompilerParams(vmem_limit_bytes=GRANT),
        )(*scalars, *arrays)

    packed_shapes = [array(sh.rim_rows), array(sh.edge_rows)] + [array(sh.message_rows)] * (n - 1)

    def along_level(x, step):
        return permute(x, "level", lambda i: sh.sends_to(i, step))

    def exchange(messages, inside):
        got = []
        for i in range(n - 1):
            got.append(along_level(messages[i], i + 1))
        got, inside = lax.optimization_barrier((got, inside))
        rim_got = sum(values[:sh.state_rim_rows] for values in got)
        return [rim_got, from_next(rim_got, "phase")] + got, inside

    other = from_next(flat, "phase")

    def in_hbm(values):
        return [pltpu.with_memory_space_constraint(v, pltpu.HBM) for v in values]

    send_plan, *outs = call(
        functools.partial(pack_kernel, sh),
        in_hbm([routes, tile_owner]),
        in_hbm([flat]),
        ([array(sh.raw_rows)] if sh.deferred else []) + [array(sh.rows)] + packed_shapes,
        3,
        [table(n - 1, PICKS + 2 * sh.slots, I32)],
        [VM((sh.rows, LANES), F32), pltpu.SemaphoreType.DMA((sh.slots,))],
        pltpu.HBM,
    )
    if sh.deferred:
        raw_got, outs = from_partner(outs[0], "src", 0), outs[1:]
    start, rims, columns, messages = outs[0], outs[1], outs[2], outs[3:]
    plan, rates, paired, rim_paired, exits = call(
        functools.partial(prep_kernel, sh),
        [routes, tile_owner, tile_levels.T, service_rates, source_rates],
        [phase_rates, batch_rates],
        [
            table((BATCH // 2 + 1) * sh.phases, 6 * full, BF16),
            table((BATCH // 2) * sh.phases, 6 * full, BF16),
            array(sh.phases),
        ],
        2,
        [table(sh.slots, ROUTES + 15, I32), table(sh.states + 1, INFLOW + SOURCES)],
        [VM((2 * full, full), F32), VM((full, LANES), F32)],
    )

    def inner(first, values, other, spans, extra=(), aliases=None):
        shapes = [array(sh.rows)]
        if spans[0][0] == "sent":
            shapes.append(array(sh.mid_rows))
        operands = [paired, exits, values, other, *extra]
        micros = 9 * sum(stop - start for _, start, stop in spans) / sh.units
        kernel = functools.partial(inner_kernel, sh, first, spans)
        return call(kernel, [plan, rates], operands, shapes, micros, aliases=aliases)

    def halo(first, inside, values, rims, columns, got, extra):
        shapes = [array(sh.rows)]
        if first:
            shapes += ([array(sh.late_rows)] if sh.deferred else []) + packed_shapes
        rims_other = from_next(rims, "phase")
        return call(
            functools.partial(halo_kernel, sh, first),
            [plan, rates] + ([send_plan] if first else []),
            [rim_paired, inside, values, rims, rims_other, columns] + got + extra,
            shapes,
            4,
        )

    if sh.deferred:
        inside, mid = inner(True, start, other, [("sent", sh.raw_end, sh.mid_end)])
        got_mid = from_partner(mid, "src", 0)
        spans = [(None, 0, sh.raw_end), (None, sh.mid_end, sh.units)]
        (inside,) = inner(True, start, other, spans, [inside], {6: 0})
        got, inside = exchange(messages, inside)
        outs = halo(True, inside, start, rims, columns, got, [raw_got])
        once, late, rims, columns, messages = outs[0], outs[1], outs[2], outs[3], outs[4:]
        got_late = from_partner(late, "src", 0)
        other = from_next(once, "phase")
        (inside,) = inner(
            False,
            once,
            other,
            [("raw", 0, sh.raw_end), ("mid", sh.raw_end, sh.mid_end), (None, sh.mid_end, sh.units)],
            [start, raw_got, got_mid],
        )
        got, inside = exchange(messages, inside)
        (twice,) = halo(False, inside, once, rims, columns, got, [])
        result = pl.pallas_call(
            functools.partial(join_kernel, sh),
            grid=(sh.slots,),
            out_shape=array(sh.rows),
            in_specs=[smem] * 2 + [vmem] * 2,
            out_specs=pl.BlockSpec((sh.rows // sh.slots, LANES), lambda k: (k, 0)),
            compiler_params=pltpu.CompilerParams(vmem_limit_bytes=GRANT),
        )(plan, rates, twice, got_late)
    else:
        (inside,) = inner(True, start, other, [(None, 0, sh.units)])
        got, inside = exchange(messages, inside)
        extra = [from_partner(start, "src", bit) for bit in range(sh.cross)]
        outs = halo(True, inside, start, rims, columns, got, extra)
        once, rims, columns, messages = outs[0], outs[1], outs[2], outs[3:]
        (inside,) = inner(False, once, from_next(once, "phase"), [(None, 0, sh.units)])
        got, inside = exchange(messages, inside)
        extra = [from_partner(once, "src", bit) for bit in range(sh.cross)]
        (result,) = halo(False, inside, once, rims, columns, got, extra)
    return result.reshape(block)


def solution(mesh):
    placed = (
        P(("groups", "level"), "src", "phase", None, None),
        P("groups", None),
        P("groups", None, None),
        P("groups"),
        P("groups", None),
        P("groups", None),
        P("groups", None),
        P("groups"),
    )

    return jax.shard_map(
        body,
        mesh=mesh,
        in_specs=placed,
        out_specs=P(("groups", "level"), "src", "phase", None, None),
        check_vma=False,
    )
```

```python
import functools

import jax
import jax.numpy as jnp
from jax import lax
from jax.experimental import pallas as pl
from jax.experimental.pallas import tpu as pltpu
from jax.sharding import PartitionSpec as P


BATCH = 16
SOURCES = 3
LANES = 128
F32 = jnp.float32
BF16 = jnp.bfloat16
I32 = jnp.int32
VM = pltpu.VMEM
SM = pltpu.SMEM
GRANT = 24 << 20
PACK_TURN = 4
GROUP = 3
GROUPS = -(-(BATCH + 1) // GROUP)

FEED, STAY, FEED_MORE, STAY_MORE, SQUARE, INFLOW = 0, 1, 2, 3, 4, 5
TILE, LEVEL_ONE, LEVEL_TWO, ROUTES = 0, 1, 2, 3
BELOW, ABOVE, LEFT, RIGHT, CORNER = 0, 1, 2, 3, 4
ROW, WANTED, LAST, PICKS = 0, 1, 2, 3


def permute(x, axis, pairs_of):
    return lax.ppermute(x, axis, [(i, pairs_of(i)) for i in range(lax.axis_size(axis))])


def from_next(x, axis):
    n = lax.axis_size(axis)
    return permute(x, axis, lambda i: (i - 1) % n)


def from_partner(x, axis, bit):
    return permute(x, axis, lambda i: i ^ 1 << bit)


class Shape:
    def __init__(self, block, tiles, levels):
        self.slots, self.states, self.phases, self.wide_two, self.wide_one = block
        self.tiles = tiles
        self.levels = levels
        self.units = self.slots * self.states
        self.rows = self.units * self.phases * self.wide_two
        self.rim_group = LANES // BATCH
        self.rim_parts = self.wide_two // self.rim_group
        self.state_rim_rows = self.states * self.rim_parts * self.phases
        self.rim_rows = self.slots * self.state_rim_rows
        self.edge_rows = self.units * self.phases
        self.lane_step = 2 * max(self.wide_two, BATCH)
        self.per_small = LANES // self.lane_step
        self.small_blocks = -(-self.states // self.per_small)
        self.small_rows_at = self.state_rim_rows + self.edge_rows
        self.message_rows = self.small_rows_at + self.small_blocks * self.phases
        self.bits = self.states.bit_length() - 1
        self.cross = SOURCES - self.bits
        self.deferred = self.cross == 1
        self.raw_end = self.states
        self.mid_end = self.units - self.states
        self.raw_rows = self.raw_end * self.wide_two * self.phases
        self.mid_rows = (self.mid_end - self.raw_end) * self.wide_two * self.phases
        self.ends_at = self.states * self.wide_two * self.phases
        self.rims_at = self.ends_at + self.mid_end * 2 * self.phases
        self.rim_units = max(self.mid_end - self.states, self.raw_end)
        self.columns_at = self.rims_at + self.rim_units * self.rim_parts * self.phases
        self.per_column = LANES // self.wide_two
        self.late_rows = self.columns_at + -(-self.mid_end // self.per_column) * self.phases
        self.power = levels & (levels - 1) == 0

    def at(self, start):
        if not isinstance(start, int):
            start = pl.multiple_of(start, self.phases)
        return pl.ds(start, self.phases)

    def native(self, unit, u):
        return pl.ds(unit * self.phases * self.wide_two + u, self.phases, stride=self.wide_two)

    def by_level(self, unit, u):
        return self.at((unit * self.wide_two + u) * self.phases)

    def rim_at(self, unit, part):
        return self.at((unit * self.rim_parts + part) * self.phases)

    def sent_rim_at(self, unit, part):
        index = unit if isinstance(unit, int) else jnp.where(unit < self.raw_end, unit, unit - self.states)
        return self.at(self.rims_at + (index * self.rim_parts + part) * self.phases)

    def small_at(self, state):
        return state // self.per_small, (state % self.per_small) * self.lane_step

    def sends_to(self, me, step):
        return me ^ step if self.power else (me + step) % self.levels

    def takes_from(self, me, step):
        return me ^ step if self.power else (me + self.levels - step) % self.levels


def sweep(start, stop, wished, visit):
    many = wished if (stop - start) % wished == 0 else 1

    def turn(index, carry):
        for j in range(many):
            visit(start + index * many + j)
        return carry

    lax.fori_loop(0, (stop - start) // many, turn, 0)


def lane_ids(shape):
    return lax.broadcasted_iota(I32, shape, len(shape) - 1)


def tile_at(owner, slot, tiles):
    found = jnp.int32(-1)
    for t in range(tiles):
        found = jnp.where(owner[t] == slot, t, found)
    return found


def route_of(routes, owner, tile, direction, slots):
    known = jnp.maximum(tile, 0)
    target = jnp.where(tile >= 0, routes[known, direction], -1)
    slot = owner[jnp.maximum(target, 0)]
    device = lax.div(slot, jnp.int32(slots))
    return target >= 0, device, slot - device * slots


def peer(sh, me, step, sending):
    if sh.power:
        return lax.bitwise_xor(me, jnp.int32(step))
    return lax.rem(me + (step if sending else sh.levels - step), jnp.int32(sh.levels))


def fill_send_plan(sh, routes, owner, plan):
    me = lax.axis_index("level")
    first = tile_at(owner, me * sh.slots, sh.tiles)
    count = jnp.int32(0)
    for k in range(sh.slots):
        count = count + jnp.where(tile_at(owner, me * sh.slots + k, sh.tiles) >= 0, 1, 0)
    for step in range(1, sh.levels):
        there = peer(sh, me, step, True)
        their_first = tile_at(owner, there * sh.slots, sh.tiles)
        lower = first < their_first
        found, device, _ = route_of(routes, owner, their_first, BELOW, sh.slots)
        plan[step - 1, ROW] = jnp.where(lower, sh.wide_two - 1, 0)
        plan[step - 1, WANTED] = jnp.where(jnp.logical_and(found, device == me), 1, 0)
        plan[step - 1, LAST] = (count - 1) * sh.states
        for k in range(sh.slots):
            tile = tile_at(owner, there * sh.slots + k, sh.tiles)
            _, _, left = route_of(routes, owner, tile, LEFT, sh.slots)
            _, _, right = route_of(routes, owner, tile, RIGHT, sh.slots)
            _, _, corner = route_of(routes, owner, tile, CORNER, sh.slots)
            plan[step - 1, PICKS + 2 * k] = jnp.where(lower, left, right) * sh.states
            plan[step - 1, PICKS + 2 * k + 1] = corner * sh.states


def add_packed(sh, lane, rims, column, u, values):
    part, q = u // sh.rim_group, u % sh.rim_group
    moved = pltpu.roll(values, (q * BATCH - (sh.wide_one - BATCH)) % LANES, 1)
    rims[part] = jnp.where(lax.div(lane, jnp.int32(BATCH)) == q, moved, rims[part])
    moved = pltpu.roll(values, u, 1) if u else values
    return jnp.where(lane == u, moved, column)


def write_messages(sh, plan, data, rims, columns, messages):
    phases, last_u = sh.phases, sh.wide_two - 1
    lane = lane_ids((phases, LANES))
    bottoms = [jnp.zeros((phases, LANES), F32) for _ in range(sh.small_blocks)]
    for s in range(sh.states):
        block, base = sh.small_at(s)
        values = columns[sh.at(s * phases), :]
        bottoms[block] = bottoms[block] + (pltpu.roll(values, base, 1) if base else values)
    for step in range(1, sh.levels):
        row = plan[step - 1, ROW]
        wanted = jnp.where(plan[step - 1, WANTED] > 0, 1.0, 0.0).astype(F32)
        last = plan[step - 1, LAST]
        for s in range(sh.states):
            for part in range(sh.rim_parts):
                messages[step - 1][sh.rim_at(s, part), :] = rims[sh.rim_at(last + s, part), :] * wanted
        small = list(bottoms)
        for k in range(sh.slots):
            slot, corner = plan[step - 1, PICKS + 2 * k], plan[step - 1, PICKS + 2 * k + 1]
            for s in range(sh.states):
                messages[step - 1][sh.at(sh.state_rim_rows + (k * sh.states + s) * phases), :] = data[sh.by_level(slot + s, row), :]
                block, base = sh.small_at(s)
                place = base + sh.lane_step // 2 + k
                moved = pltpu.roll(columns[sh.at((corner + s) * phases), :], (place - last_u) % LANES, 1)
                small[block] = jnp.where(lane == place, moved, small[block])
        for i, values in enumerate(small):
            messages[step - 1][sh.at(sh.small_rows_at + i * phases), :] = values


def pack_kernel(sh, routes, owner, data_hbm, send_plan, *outs):
    outs, (data, arrived) = outs[:-2], outs[-2:]
    raw, (by_level, rims, columns, *messages) = (outs[0], outs[1:]) if sh.deferred else (None, outs)
    lane = lane_ids((sh.phases, LANES))
    size = sh.rows // sh.slots
    copies = [
        pltpu.make_async_copy(data_hbm.at[pl.ds(k * size, size)], data.at[pl.ds(k * size, size)], arrived.at[k])
        for k in range(sh.slots)
    ]
    for copy in copies:
        copy.start()
    fill_send_plan(sh, routes, owner, send_plan)

    def reorder(to_src, unit):
        packed = [jnp.zeros((sh.phases, LANES), F32) for _ in range(sh.rim_parts)]
        column = jnp.zeros((sh.phases, LANES), F32)
        for u in range(sh.wide_two):
            values = data[sh.native(unit, u), :]
            by_level[sh.by_level(unit, u), :] = values
            if to_src:
                raw[sh.by_level(unit, u), :] = values
            column = add_packed(sh, lane, packed, column, u, values)
        for part, values in enumerate(packed):
            rims[sh.rim_at(unit, part), :] = values
        columns[sh.at(unit * sh.phases), :] = column

    for k, copy in enumerate(copies):
        copy.wait()
        sweep(k * sh.states, (k + 1) * sh.states, PACK_TURN, functools.partial(reorder, sh.deferred and k == 0))
    write_messages(sh, send_plan, by_level, rims, columns, messages)


def source_scalars(sources, scale, state):
    feed = jnp.float32(0.0)
    outflow = jnp.float32(0.0)
    inflow = []
    for k in range(SOURCES):
        on = lax.rem(lax.shift_right_logical(state, jnp.int32(k)), jnp.int32(2)) == 1
        turn_on, turn_off, arrive = sources[k, 0], sources[k, 1], sources[k, 2]
        feed = feed + jnp.where(on, arrive, 0.0)
        outflow = outflow + jnp.where(on, turn_off, turn_on)
        inflow.append(jnp.where(on, turn_on, turn_off) * scale)
    return feed * scale, outflow * scale, inflow


def prep_kernel(sh, routes, owner, levels_t, service, sources, phase_rates, batch_rates, plan, rates, paired, rim_paired,
                exits, turned, wide):
    me = lax.axis_index("level")
    for k in range(sh.slots):
        tile = tile_at(owner, me * sh.slots + k, sh.tiles)
        known = jnp.maximum(tile, 0)
        plan[k, TILE] = tile
        plan[k, LEVEL_ONE] = levels_t[0, known]
        plan[k, LEVEL_TWO] = levels_t[1, known]
        for r in range(5):
            found, device, slot = route_of(routes, owner, tile, r, sh.slots)
            kind = jnp.int32(1)
            for step in range(1, sh.levels):
                kind = jnp.where(device == peer(sh, me, step, False), step + 1, kind)
            plan[k, ROUTES + 3 * r] = jnp.where(found, kind, 0)
            plan[k, ROUTES + 3 * r + 1] = slot * sh.states
            plan[k, ROUTES + 3 * r + 2] = jnp.where(slot == 0, 1, 0)

    phases, full = sh.phases, phase_rates.shape[0]
    start = lax.axis_index("phase") * phases
    rows_here = pl.ds(pl.multiple_of(start, phases), phases)
    shape = (full, full)
    moving = phase_rates[...]
    moving = jnp.where(lax.broadcasted_iota(I32, shape, 0) == lax.broadcasted_iota(I32, shape, 1), 0.0, moving)
    total = moving
    for b in range(BATCH):
        total = total + batch_rates[b]
    leaving = jnp.sum(total, axis=1, keepdims=True)
    sources_top = jnp.float32(0.0)
    for k in range(SOURCES):
        sources_top = sources_top + jnp.maximum(sources[k, 2] + sources[k, 1], sources[k, 0])
    uniform = jnp.max(leaving) + (service[0] + service[1] + sources_top)
    inverse = 1.0 / jnp.full((phases, LANES), uniform, F32)
    scale = jnp.max(inverse)
    wide[...] = jnp.broadcast_to(leaving, (full, LANES))
    exits[...] = wide[rows_here, :] * inverse

    base = lax.axis_index("src") * sh.states
    rates[sh.states, 0] = service[0] * scale
    rates[sh.states, 1] = service[1] * scale
    for s in range(sh.states):
        state = base + s
        feed, outflow, inflow = source_scalars(sources, scale, state)
        rates[s, FEED] = feed
        rates[s, STAY] = 1.0 - feed - outflow
        for k in range(SOURCES):
            rates[s, INFLOW + k] = inflow[k]
        if sh.deferred:
            there = lax.bitwise_xor(state, jnp.int32(1 << sh.bits))
            feed_there, outflow_there, inflow_there = source_scalars(sources, scale, there)
            rates[s, FEED_MORE] = feed_there - feed
            rates[s, STAY_MORE] = (feed + outflow) - (feed_there + outflow_there)
            rates[s, SQUARE] = inflow[sh.bits] * inflow_there[sh.bits]

    for b in range(GROUP * GROUPS):
        if b <= BATCH:
            values = (moving if b == 0 else batch_rates[b - 1]) * scale
            turned[0:full, :] = values
            turned[full:2 * full, :] = values
            turned[0:full, :] = turned[pl.ds(pl.multiple_of(start, phases), full), :].T
            values = turned[rows_here, :]
            high = values.astype(BF16)
            low = (values - high.astype(F32)).astype(BF16)
        else:
            high = jnp.zeros((phases, full), BF16)
            low = high
        parts = (high, low, high)
        for i, part in enumerate(parts):
            if 1 <= b <= BATCH:
                column = ((b - 1) % 2) * 3 * full + i * full
                rim_paired[((b - 1) // 2) * phases:((b - 1) // 2 + 1) * phases, column:column + full] = part
            column = (b % GROUP) * 3 * full + i * full
            paired[(b // GROUP) * phases:(b // GROUP + 1) * phases, column:column + full] = part


def split(values):
    high = values.astype(BF16)
    low = (values - high.astype(F32)).astype(BF16)
    return [high, high, low]


def inner_kernel(sh, first, spans, plan, rates, weights, exits, own, other, *refs):
    phases = sh.phases
    start_values, raw_got, got_mid = refs[:3] if sh.deferred and not first else (None, None, None)
    out, sent = refs[-2:] if spans[0][0] == "sent" else (refs[-1], None)
    other_at = sh.native if first else sh.by_level
    serve_one, serve_two = rates[sh.states, 0], rates[sh.states, 1]
    lane = lane_ids((phases, LANES))
    inner_one = jnp.where(lane == LANES - 1, 0.0, serve_one)
    level = lane_ids((weights.shape[1] // (3 * GROUP), LANES))

    def unit_step(group, unit):
        k = lax.div(unit, jnp.int32(sh.states))
        s = unit - k * sh.states
        a, c = plan[k, LEVEL_ONE], plan[k, LEVEL_TWO]
        feed = rates[s, FEED]
        stay = rates[s, STAY] - exits[...] - jnp.where(jnp.logical_or(lane > 0, a > 0), serve_one, 0.0)
        for pair in range(sh.wide_two // 2):
            columns = []
            for u in (2 * pair, 2 * pair + 1):
                values = jnp.concatenate([own[sh.by_level(unit, u), :], other[other_at(unit, u), :]], axis=0)
                parts = split(values)
                for e in range(1, GROUP):
                    parts += split(jnp.where(level >= e, pltpu.roll(values, e, 1), 0.0))
                columns.append(jnp.concatenate(parts, axis=0))
            product = jnp.dot(weights[...], jnp.concatenate(columns, axis=1), preferred_element_type=F32)
            for j, u in enumerate((2 * pair, 2 * pair + 1)):
                lanes = slice(j * LANES, (j + 1) * LANES)
                total = product[0:phases, lanes]
                for b in range(1, GROUPS):
                    moved = pltpu.roll(product[b * phases:(b + 1) * phases, lanes], GROUP * b, 1)
                    total = total + jnp.where(lane >= GROUP * b, moved, 0.0)
                here = own[sh.by_level(unit, u), :]
                two = serve_two if u else jnp.where(c > 0, serve_two, 0.0)
                total = total + (stay - two) * here
                if u:
                    prev = own[sh.by_level(unit, u - 1), :]
                    total = total + inner_one * pltpu.roll(prev, LANES - 1, 1) + feed * prev
                if u + 1 < sh.wide_two:
                    total = total + serve_two * own[sh.by_level(unit, u + 1), :]
                for bit in range(sh.bits):
                    flipped = unit - s + lax.bitwise_xor(s, jnp.int32(1 << bit))
                    total = total + rates[s, INFLOW + bit] * own[sh.by_level(flipped, u), :]
                if start_values is not None:
                    total = total + rates[s, SQUARE] * start_values[sh.by_level(unit, u), :]
                    if group == "raw":
                        more = rates[s, STAY_MORE] * raw_got[sh.by_level(unit, u), :]
                        if u:
                            more = more + rates[s, FEED_MORE] * raw_got[sh.by_level(unit, u - 1), :]
                        total = total + rates[s, INFLOW + sh.bits] * more
                    if group == "mid":
                        total = total + rates[s, INFLOW + sh.bits] * got_mid[sh.by_level(unit - sh.raw_end, u), :]
                out[sh.by_level(unit, u), :] = total
                if group == "sent":
                    more = rates[s, STAY_MORE] * here
                    if u:
                        more = more + rates[s, FEED_MORE] * prev
                    sent[sh.by_level(unit - sh.raw_end, u), :] = 2.0 * total + more

    for group, start, stop in spans:
        sweep(start, stop, 2, functools.partial(unit_step, group))


def halo_kernel(sh, first, *refs):
    refs = list(refs)
    n, phases, last_u = sh.levels, sh.phases, sh.wide_two - 1
    plan, rates = refs[:2]
    refs = refs[2:]
    send_plan = refs.pop(0) if first else None
    weights, inner, own, rims_own, rims_other, columns_own, rim_got, rim_other = refs[:8]
    refs = refs[8:]
    edges, refs = refs[:n - 1], refs[n - 1:]
    raw = 0 if sh.deferred else sh.cross
    partners, refs = refs[:raw], refs[raw:]
    raw_got = refs.pop(0) if sh.deferred and first else None
    out = refs.pop(0)
    sent = refs.pop(0) if sh.deferred and first else None
    rims_out, columns_out = (refs.pop(0), refs.pop(0)) if first else (None, None)
    serve_one, serve_two = rates[sh.states, 0], rates[sh.states, 1]
    lane = lane_ids((phases, LANES))
    group_lane = lax.rem(lane, jnp.int32(BATCH))
    zero = jnp.zeros((phases, LANES), F32)
    if sent is not None:
        for start in range(sh.columns_at, sh.late_rows, phases):
            sent[start:start + phases, :] = zero

    def rim_product(halves):
        columns = []
        for pair in halves:
            values = jnp.concatenate(pair, axis=0)
            ends = lax.rem(lane_ids(values.shape), jnp.int32(BATCH)) == BATCH - 1
            moved = jnp.where(ends, 0.0, pltpu.roll(values, LANES - 1, 1))
            columns.append(jnp.concatenate(split(moved) + split(values), axis=0))
        product = jnp.dot(weights[...], jnp.concatenate(columns, axis=1), preferred_element_type=F32)
        sums = []
        for i in range(len(halves)):
            total = product[(BATCH // 2 - 1) * phases:(BATCH // 2) * phases, i * LANES:(i + 1) * LANES]
            for j in range(BATCH // 2 - 1):
                block = product[j * phases:(j + 1) * phases, i * LANES:(i + 1) * LANES]
                moved = pltpu.roll(block, (2 * j + 2 - BATCH) % LANES, 1)
                total = total + jnp.where(group_lane <= 2 * j + 1, moved, 0.0)
            sums.append(total)
        return sums

    def unit_step(group, unit):
        k = lax.div(unit, jnp.int32(sh.states))
        s = unit - k * sh.states

        def kind(which):
            return plan[k, ROUTES + 3 * which]

        def beside(which):
            return plan[k, ROUTES + 3 * which + 1] + s

        def kept(which):
            return jnp.where(plan[k, ROUTES + 3 * which + 2] > 0, 0.0, 1.0).astype(F32)

        def number(flag):
            return jnp.where(flag, 1.0, 0.0).astype(F32)

        def remote(which, rows):
            value = zero
            for step in range(1, n):
                value = jnp.where(kind(which) == step + 1, edges[step - 1][rows, :], value)
            return value

        small_base = lax.rem(s, jnp.int32(sh.per_small)) * sh.lane_step
        small_at = sh.at(sh.small_rows_at + lax.div(s, jnp.int32(sh.per_small)) * phases)
        edge_at = sh.at(sh.state_rim_rows + unit * phases)
        left = jnp.where(kind(LEFT) == 1, own[sh.by_level(beside(LEFT), last_u), :], remote(LEFT, edge_at))
        right = jnp.where(kind(RIGHT) == 1, own[sh.by_level(beside(RIGHT), 0), :], remote(RIGHT, edge_at))
        above = jnp.where(
            kind(ABOVE) == 1,
            columns_own[sh.at(beside(ABOVE) * phases), :],
            pltpu.roll(remote(ABOVE, small_at), LANES - small_base, 1),
        )
        above = jnp.where(lane < sh.wide_two, above, 0.0) * serve_one
        corner = jnp.where(
            kind(CORNER) == 1,
            pltpu.roll(columns_own[sh.at(beside(CORNER) * phases), :], LANES - 1 - last_u, 1),
            pltpu.roll(remote(CORNER, small_at), LANES - 1 - (small_base + sh.lane_step // 2 + k), 1),
        )
        corner = jnp.where(lane == LANES - 1, corner, 0.0) * serve_one
        shifted = jnp.where(lane == LANES - 1, 0.0, pltpu.roll(left, LANES - 1, 1)) * serve_one
        below_local, below_remote = number(kind(BELOW) == 1), number(kind(BELOW) > 1)
        under = []
        for part in range(sh.rim_parts):
            under.append([
                rims_own[sh.rim_at(beside(BELOW), part), :] * below_local + rim_got[sh.rim_at(s, part), :] * below_remote,
                rims_other[sh.rim_at(beside(BELOW), part), :] * below_local
                + rim_other[sh.rim_at(s, part), :] * below_remote,
            ])
        feed = rates[s, FEED]
        rims = rim_product(under)
        if group is not None:
            keep_left = kept(LEFT)
            rim_scale, column_scale = 2.0 * kept(BELOW), 2.0 * kept(ABOVE)
            sent_first = (2.0 * keep_left) * (shifted + feed * left) + (2.0 * kept(CORNER)) * corner
            sent_first = sent_first + ((2.0 * keep_left - 1.0) * rates[s, FEED_MORE]) * left
            sent_last = (2.0 * kept(RIGHT) * serve_two) * right
            if group != "last":
                sent[sh.at(sh.ends_at + 2 * unit * phases), :] = sent_first
                sent[sh.at(sh.ends_at + (2 * unit + 1) * phases), :] = sent_last
                if group != "second":
                    for part in range(sh.rim_parts):
                        sent[sh.sent_rim_at(unit, part), :] = rim_scale * rims[part]
                place = sh.at(sh.columns_at + lax.div(unit, jnp.int32(sh.per_column)) * phases)
                base = lax.rem(unit, jnp.int32(sh.per_column)) * sh.wide_two
                sent[place, :] = sent[place, :] + column_scale * pltpu.roll(above, base, 1)
        packed, packed_column = [zero] * sh.rim_parts, zero
        for u in range(sh.wide_two):
            part, q = u // sh.rim_group, u % sh.rim_group

            inside = inner[sh.by_level(unit, u), :]
            rim = jnp.where(lane < BATCH, pltpu.roll(rims[part], LANES - q * BATCH, 1) if q else rims[part], 0.0)
            edge = jnp.where(lane == LANES - 1, pltpu.roll(above, LANES - u, 1), 0.0) if u else zero
            total = inside + rim + edge
            if u == 0:
                total = total + shifted + corner + feed * left
            if u == last_u:
                total = total + serve_two * right
            for bit, values in enumerate(partners):
                total = total + rates[s, INFLOW + sh.bits + bit] * values[sh.by_level(unit, u), :]
            if group == "raw":
                total = total + (2.0 * rates[s, INFLOW + sh.bits]) * raw_got[sh.by_level(unit, u), :]
            if first:
                packed_column = add_packed(sh, lane, packed, packed_column, u, total)
            if first or sh.deferred:
                out[sh.by_level(unit, u), :] = total
            else:
                out[sh.native(unit, u), :] = jnp.where(plan[k, TILE] >= 0, total, 0.0)
            if group == "last":
                value = 2.0 * inside + rim_scale * rim + column_scale * edge
                value = value + rates[s, STAY_MORE] * own[sh.by_level(unit, u), :]
                if u:
                    value = value + rates[s, FEED_MORE] * own[sh.by_level(unit, u - 1), :]
                else:
                    value = value + sent_first
                if u == last_u:
                    value = value + sent_last
                sent[sh.by_level(unit - sh.mid_end, u), :] = value
        if first:
            for part in range(sh.rim_parts):
                rims_out[sh.rim_at(unit, part), :] = packed[part]
            columns_out[sh.at(unit * phases), :] = packed_column

    turn = 2 if first else 4

    if sent is not None:
        sweep(0, sh.raw_end, turn, functools.partial(unit_step, "raw"))
        second_end = min(2 * sh.states, sh.mid_end)
        sweep(sh.raw_end, second_end, turn, functools.partial(unit_step, "second"))
        if sh.mid_end > second_end:
            sweep(second_end, sh.mid_end, turn, functools.partial(unit_step, "mid"))
        sweep(sh.mid_end, sh.units, turn, functools.partial(unit_step, "last"))
    else:
        sweep(0, sh.units, turn, functools.partial(unit_step, None))
    if first:
        write_messages(sh, send_plan, out, rims_out, columns_out, refs)


def join_kernel(sh, plan, rates, stepped, got_late, out):
    phases, last_u = sh.phases, sh.wide_two - 1
    lane = lane_ids((phases, LANES))
    inflow = rates[0, INFLOW + sh.bits]
    slot = pl.program_id(0)
    filled = plan[slot, TILE] >= 0

    def unit_step(group, state):
        unit = slot * sh.states + state
        if group != "last":
            column = got_late[sh.at(sh.columns_at + lax.div(unit, jnp.int32(sh.per_column)) * phases), :]
            base = lax.rem(unit, jnp.int32(sh.per_column)) * sh.wide_two
        if group == "rims":
            rims = [got_late[sh.sent_rim_at(unit, part), :] for part in range(sh.rim_parts)]
        for u in range(sh.wide_two):
            if group == "last":
                got = got_late[sh.by_level(unit - sh.mid_end, u), :]
            else:
                got = jnp.zeros((phases, LANES), F32)
                if group == "rims":
                    part, q = u // sh.rim_group, u % sh.rim_group
                    got = jnp.where(lane < BATCH, pltpu.roll(rims[part], LANES - q * BATCH, 1) if q else rims[part], 0.0)
                if u:
                    got = jnp.where(lane == LANES - 1, pltpu.roll(column, LANES - (base + u), 1), got)
                if u in (0, last_u):
                    got = got + got_late[sh.at(sh.ends_at + (2 * unit + (1 if u else 0)) * phases), :]
            total = stepped[sh.by_level(unit, u), :] + inflow * got
            out[sh.native(state, u), :] = jnp.where(filled, total, 0.0)

    def slot_step(group):
        sweep(0, sh.states, 4, functools.partial(unit_step, group))

    last = slot == sh.slots - 1
    second = jnp.logical_and(slot == 1, jnp.logical_not(last))
    pl.when(last)(functools.partial(slot_step, "last"))
    pl.when(second)(functools.partial(slot_step, "second"))
    pl.when(jnp.logical_not(jnp.logical_or(last, second)))(functools.partial(slot_step, "rims"))


def body(
    state_values,
    phase_rates,
    batch_rates,
    service_rates,
    source_rates,
    tile_levels,
    routes,
    tile_owner,
):
    block = state_values.shape
    sh = Shape(block, tile_owner.shape[0], lax.axis_size("level"))
    n, full = sh.levels, phase_rates.shape[0]
    flat = state_values.reshape(sh.rows, LANES)
    smem, vmem = pl.BlockSpec(memory_space=SM), pl.BlockSpec(memory_space=VM)

    def array(rows):
        return jax.ShapeDtypeStruct((rows, LANES), F32)

    def table(rows, columns, dtype=F32):
        return jax.ShapeDtypeStruct((rows, columns), dtype)

    def call(kernel, scalars, arrays, shapes, micros, scalar_shapes=(), scratch=(), space=VM, aliases=None):
        return pl.pallas_call(
            kernel,
            out_shape=tuple(scalar_shapes) + tuple(shapes),
            in_specs=[smem] * len(scalars) + [pl.BlockSpec(memory_space=space)] * len(arrays),
            out_specs=tuple([smem] * len(scalar_shapes) + [vmem] * len(shapes)),
            scratch_shapes=list(scratch),
            input_output_aliases=aliases or {},
            cost_estimate=pl.CostEstimate(flops=0, bytes_accessed=int(micros * 3.0e6), transcendentals=0),
            compiler_params=pltpu.CompilerParams(vmem_limit_bytes=GRANT),
        )(*scalars, *arrays)

    packed_shapes = [array(sh.rim_rows), array(sh.edge_rows)] + [array(sh.message_rows)] * (n - 1)

    def along_level(x, step):
        return permute(x, "level", lambda i: sh.sends_to(i, step))

    def exchange(messages, inside):
        got = []
        for i in range(n - 1):
            got.append(along_level(messages[i], i + 1))
        got, inside = lax.optimization_barrier((got, inside))
        rim_got = sum(values[:sh.state_rim_rows] for values in got)
        return [rim_got, from_next(rim_got, "phase")] + got, inside

    other = from_next(flat, "phase")

    def in_hbm(values):
        return [pltpu.with_memory_space_constraint(v, pltpu.HBM) for v in values]

    send_plan, *outs = call(
        functools.partial(pack_kernel, sh),
        in_hbm([routes, tile_owner]),
        in_hbm([flat]),
        ([array(sh.raw_rows)] if sh.deferred else []) + [array(sh.rows)] + packed_shapes,
        3,
        [table(n - 1, PICKS + 2 * sh.slots, I32)],
        [VM((sh.rows, LANES), F32), pltpu.SemaphoreType.DMA((sh.slots,))],
        pltpu.HBM,
    )
    if sh.deferred:
        raw_got, outs = from_partner(outs[0], "src", 0), outs[1:]
    start, rims, columns, messages = outs[0], outs[1], outs[2], outs[3:]
    plan, rates, paired, rim_paired, exits = call(
        functools.partial(prep_kernel, sh),
        [routes, tile_owner, tile_levels.T, service_rates, source_rates],
        [phase_rates, batch_rates],
        [
            table(GROUPS * sh.phases, 3 * GROUP * full, BF16),
            table((BATCH // 2) * sh.phases, 6 * full, BF16),
            array(sh.phases),
        ],
        2,
        [table(sh.slots, ROUTES + 15, I32), table(sh.states + 1, INFLOW + SOURCES)],
        [VM((2 * full, full), F32), VM((full, LANES), F32)],
    )

    def inner(first, values, other, spans, extra=(), aliases=None):
        shapes = [array(sh.rows)]
        if spans[0][0] == "sent":
            shapes.append(array(sh.mid_rows))
        operands = [paired, exits, values, other, *extra]
        micros = 9 * sum(stop - start for _, start, stop in spans) / sh.units
        kernel = functools.partial(inner_kernel, sh, first, spans)
        return call(kernel, [plan, rates], operands, shapes, micros, aliases=aliases)

    def halo(first, inside, values, rims, columns, got, extra):
        shapes = [array(sh.rows)]
        if first:
            shapes += ([array(sh.late_rows)] if sh.deferred else []) + packed_shapes
        rims_other = from_next(rims, "phase")
        return call(
            functools.partial(halo_kernel, sh, first),
            [plan, rates] + ([send_plan] if first else []),
            [rim_paired, inside, values, rims, rims_other, columns] + got + extra,
            shapes,
            4,
        )

    if sh.deferred:
        inside, mid = inner(True, start, other, [("sent", sh.raw_end, sh.mid_end)])
        got_mid = from_partner(mid, "src", 0)
        spans = [(None, 0, sh.raw_end), (None, sh.mid_end, sh.units)]
        (inside,) = inner(True, start, other, spans, [inside], {6: 0})
        got, inside = exchange(messages, inside)
        outs = halo(True, inside, start, rims, columns, got, [raw_got])
        once, late, rims, columns, messages = outs[0], outs[1], outs[2], outs[3], outs[4:]
        got_late = from_partner(late, "src", 0)
        other = from_next(once, "phase")
        (inside,) = inner(
            False,
            once,
            other,
            [("raw", 0, sh.raw_end), ("mid", sh.raw_end, sh.mid_end), (None, sh.mid_end, sh.units)],
            [start, raw_got, got_mid],
        )
        got, inside = exchange(messages, inside)
        (twice,) = halo(False, inside, once, rims, columns, got, [])
        result = pl.pallas_call(
            functools.partial(join_kernel, sh),
            grid=(sh.slots,),
            out_shape=array(sh.rows),
            in_specs=[smem] * 2 + [vmem] * 2,
            out_specs=pl.BlockSpec((sh.rows // sh.slots, LANES), lambda k: (k, 0)),
            compiler_params=pltpu.CompilerParams(vmem_limit_bytes=GRANT),
        )(plan, rates, twice, got_late)
    else:
        (inside,) = inner(True, start, other, [(None, 0, sh.units)])
        got, inside = exchange(messages, inside)
        extra = [from_partner(start, "src", bit) for bit in range(sh.cross)]
        outs = halo(True, inside, start, rims, columns, got, extra)
        once, rims, columns, messages = outs[0], outs[1], outs[2], outs[3:]
        (inside,) = inner(False, once, from_next(once, "phase"), [(None, 0, sh.units)])
        got, inside = exchange(messages, inside)
        extra = [from_partner(once, "src", bit) for bit in range(sh.cross)]
        (result,) = halo(False, inside, once, rims, columns, got, extra)
    return result.reshape(block)


def solution(mesh):
    placed = (
        P(("groups", "level"), "src", "phase", None, None),
        P("groups", None),
        P("groups", None, None),
        P("groups"),
        P("groups", None),
        P("groups", None),
        P("groups", None),
        P("groups"),
    )

    return jax.shard_map(
        body,
        mesh=mesh,
        in_specs=placed,
        out_specs=P(("groups", "level"), "src", "phase", None, None),
        check_vma=False,
    )
```
